256 devices in a mesh: tgt: 4 (over z_lo, core), sup: 64 (over y, x, z_hi).
Axes of the slice: x: 4, y: 4, z: 8 (z_hi: 4, z_lo: 2; z = z_hi * 2 + z_lo), core: 2. Of those that a mesh axis runs over, the one named last changes fastest.
Arguments:
- support_images: bfloat16 [512, 3072], P('sup'), may hold values from -6 to 6
- target_images: bfloat16 [262144, 3072], P(('tgt', 'sup')), may hold values from -6 to 6
- support_labels: int32 [512], replicated, may hold values from 0 to 99
- target_labels: int32 [262144], P(('tgt', 'sup')), may hold values from 0 to 99
Outputs:
- scaled_grad: float32 [512, 3072], P('sup')
- loss: float32 [], replicated
The draws below stay inside these ranges and needn't reach their ends.
All inputs are finite; a program needn't handle non-finite values.
Results may differ from the reference program's by a relative error of at most 0.0095.
Values may be sent and summed in bfloat16 or wider, within the bound.
A program may use at most 128 MiB of HBM per device.

```python
import math
import jax
import jax.numpy as jnp
from jax import lax

D = 3072
C = 100
LAYERS = 5
SUPPORT = 512
TARGETS = 262144
N_SUP = 64


def shared_parts(key):
    base_key = jax.random.fold_in(key, 7001)
    mean_image = jax.random.normal(jax.random.fold_in(base_key, 1), (D,), jnp.float32)
    proto_count = 48
    prototypes = jax.random.normal(jax.random.fold_in(base_key, 2), (proto_count, D), jnp.float32)
    return (mean_image, prototypes)


def draw_images(key, row_count, salt_value):
    mean_image, prototypes = shared_parts(key)
    own_key = jax.random.fold_in(key, salt_value)
    subkeys = jax.random.split(own_key, 4)
    chosen = jax.random.randint(subkeys[0], (row_count, 4), 0, prototypes.shape[0])
    mix_weights = 0.45 * jax.random.normal(subkeys[1], (row_count, 4), jnp.float32)
    mean_weight = jax.random.uniform(subkeys[2], (row_count, 1), jnp.float32, 0.2, 1.4)
    rough = 0.45 * jax.random.normal(subkeys[3], (row_count, D), jnp.float32)
    images = mean_weight * mean_image[None, :] + rough
    for slot_no in range(4):
        images = images + mix_weights[:, slot_no:slot_no + 1] * prototypes[chosen[:, slot_no]]
    return jnp.clip(images, -6.0, 6.0).astype(jnp.bfloat16)


def draw_support_images(key, part):
    return draw_images(key, SUPPORT, 11)


def draw_target_images(key, part):
    return draw_images(key, TARGETS, 12)


def touch_ends(array, key, low, high):
    spot = [jax.random.randint(jax.random.fold_in(key, axis), (), 0, length) for axis, length in enumerate(array.shape)]
    main_axis = array.shape.index(max(array.shape))
    beside = spot[:main_axis] + [(spot[main_axis] + 1) % array.shape[main_axis]] + spot[main_axis + 1:]
    return array.at[tuple(spot)].set(low).at[tuple(beside)].set(high)


def setup_inputs(seed: int = 0) -> dict:
    key_of = jax.random.split(jax.random.key(seed), 5)
    return {
        "support_images": draw_support_images(jax.random.fold_in(key_of[4], 71), 0),
        "target_images": draw_target_images(jax.random.fold_in(key_of[4], 71), 0),
        "support_labels": touch_ends(jax.random.randint(key_of[2], (SUPPORT,), 0, C), jax.random.fold_in(key_of[2], 1), 0, C - 1).astype(jnp.int32),
        "target_labels": touch_ends(jax.random.randint(key_of[3], (TARGETS,), 0, C), jax.random.fold_in(key_of[3], 1), 0, C - 1).astype(jnp.int32),
    }


ridge_scale = 0.1
two_over_pi = 2.0 / math.pi

def ntk_kernel(gram_in, norm_row, norm_col):
    tangent = gram_in
    for layer_no in range(LAYERS):
        spread = (1.0 + 2.0 * norm_row) * (1.0 + 2.0 * norm_col)
        new_gram = two_over_pi * jnp.arcsin(2.0 * gram_in / jnp.sqrt(spread))
        slope_term = 2.0 * two_over_pi / jnp.sqrt(spread - 4.0 * gram_in * gram_in)
        tangent = new_gram + tangent * slope_term
        norm_row = two_over_pi * jnp.arcsin(2.0 * norm_row / (1.0 + 2.0 * norm_row))
        norm_col = two_over_pi * jnp.arcsin(2.0 * norm_col / (1.0 + 2.0 * norm_col))
        gram_in = new_gram
    return tangent

def ridge_solve(factor, rhs_block):
    middle = lax.linalg.triangular_solve(factor, rhs_block, left_side=True, lower=True)
    return lax.linalg.triangular_solve(factor, middle, left_side=True, lower=True, transpose_a=True)

def reference(support_images, target_images, support_labels, target_labels):
    contract = (((1,), (1,)), ((), ()))
    back_dims = (((0,), (0,)), ((), ()))
    sup_count = support_images.shape[0]
    total_tgt = target_images.shape[0]
    block_rows = total_tgt // N_SUP
    norm_sup = lax.optimization_barrier(jnp.sum(jnp.square(support_images.astype(jnp.float32)), axis=1)) / D
    gram_ss = lax.dot_general(support_images.astype(jnp.float32), support_images.astype(jnp.float32), contract, preferred_element_type=jnp.float32) / D
    kern_ss, pull_ss = jax.vjp(ntk_kernel, gram_ss, norm_sup[:, None], norm_sup[None, :])
    trace_mean = jnp.trace(kern_ss) / sup_count
    system = kern_ss + ridge_scale * trace_mean * jnp.eye(sup_count, dtype=jnp.float32)
    factor = jnp.linalg.cholesky(system)
    classes = jnp.arange(C, dtype=jnp.int32)
    label_sup = (support_labels[:, None] == classes[None, :]).astype(jnp.float32) - 1.0 / C
    coeffs = ridge_solve(factor, label_sup)

    def one_block(carry, pieces):
        d_coeffs, loss_sum, pixel_grad, norm_grad = carry
        images, labels = pieces
        norm_tgt = lax.optimization_barrier(jnp.sum(jnp.square(images.astype(jnp.float32)), axis=1)) / D
        gram_ts = lax.dot_general(images.astype(jnp.float32), support_images.astype(jnp.float32), contract, preferred_element_type=jnp.float32) / D
        kern_ts, pull_ts = jax.vjp(ntk_kernel, gram_ts, norm_tgt[:, None], norm_sup[None, :])
        label_tgt = (labels[:, None] == classes[None, :]).astype(jnp.float32) - 1.0 / C
        misfit = jnp.dot(kern_ts, coeffs, precision=lax.Precision.HIGHEST) - label_tgt
        d_predict = misfit / total_tgt
        d_coeffs = d_coeffs + jnp.dot(kern_ts.T, d_predict, precision=lax.Precision.HIGHEST)
        loss_sum = loss_sum + jnp.sum(misfit * misfit)
        d_kern_ts = jnp.dot(d_predict, coeffs.T, precision=lax.Precision.HIGHEST)
        g_ts, unused_tgt, qcol_ts = pull_ts(d_kern_ts)
        coef_ts = (g_ts / D).astype(jnp.bfloat16)
        pixel_grad = pixel_grad + lax.dot_general(coef_ts.astype(jnp.float32), images.astype(jnp.float32), back_dims, preferred_element_type=jnp.float32)
        norm_grad = norm_grad + qcol_ts[0]
        return ((d_coeffs, loss_sum, pixel_grad, norm_grad), None)
    init = (jnp.zeros((sup_count, C), jnp.float32), jnp.zeros((), jnp.float32), jnp.zeros((sup_count, D), jnp.float32), jnp.zeros((sup_count,), jnp.float32))
    image_blocks = target_images.reshape(N_SUP, block_rows, D)
    label_blocks = target_labels.reshape(N_SUP, block_rows)
    totals, unused_out = lax.scan(one_block, init, (image_blocks, label_blocks))
    d_coeffs, loss_sum, pixel_grad, norm_grad = totals
    loss_value = loss_sum / (2.0 * total_tgt)
    adjoint = ridge_solve(factor, d_coeffs)
    ridge_grad = -ridge_scale / sup_count * jnp.sum(adjoint * coeffs)
    d_kern_ss = -jnp.dot(adjoint, coeffs.T, precision=lax.Precision.HIGHEST) + ridge_grad * jnp.eye(sup_count, dtype=jnp.float32)
    g_ss, qrow_ss, qcol_ss = pull_ss(d_kern_ss)
    coef_ss = (g_ss / D).astype(jnp.bfloat16)
    pixel_grad = pixel_grad + lax.dot_general(coef_ss.astype(jnp.float32), support_images.astype(jnp.float32), back_dims, preferred_element_type=jnp.float32)
    pixel_grad = pixel_grad + jnp.dot(coef_ss.astype(jnp.float32), support_images.astype(jnp.float32), preferred_element_type=jnp.float32)
    norm_grad = norm_grad + qcol_ss[0] + qrow_ss[:, 0]
    pixel_grad = pixel_grad + 2.0 / D * norm_grad[:, None] * support_images.astype(jnp.float32)
    return (sup_count * pixel_grad, loss_value)
```

```python
import functools
import math

import jax
import jax.numpy as jnp
from jax import lax
from jax.experimental import pallas as pl
from jax.experimental.pallas import tpu as pltpu
from jax.sharding import PartitionSpec as P

D = 3072
C = 100
LAYERS = 5
CLS = 128
RIDGE = 0.1
TWO_PI = 2.0 / math.pi
NEWTON = 7
REFINE = 3
HI = lax.Precision.HIGHEST
NN = (((1,), (0,)), ((), ()))
NT = (((1,), (1,)), ((), ()))
F32 = jnp.float32
BF16 = jnp.bfloat16

ASIN = (
    (1.0, 0.1666678637266159, 0.0749453455209732, 0.0455390103161335, 0.02390936389565468, 0.042553599923849106),
    (1.0, 0.16666781902313232, 0.07494797557592392, 0.04552660509943962, 0.02313542366027832, 0.0537058524787426, -0.05348314717411995, 0.08573318272829056),
    (1.0, 0.16666752099990845, 0.07495901733636856, 0.04535885155200958, 0.024863531813025475, 0.04080614075064659),
    (1.0, 0.16666492819786072, 0.0750882476568222, 0.043096426874399185, 0.04107564687728882),
    (1.0, 0.16666613519191742, 0.07503537833690643, 0.043817341327667236, 0.03804752230644226),
)


def poly(z, coefs):
    total = coefs[-1] * TWO_PI
    for value in coefs[-2::-1]:
        total = total * z + value * TWO_PI
    return total


def scaled_asin(layer, u, u2):
    if layer > 0:
        return u * poly(u2, ASIN[layer])
    size = jnp.abs(u)
    big = size > 0.5
    z = jnp.where(big, 0.5 - 0.5 * size, u2)
    s = jnp.where(big, z * lax.rsqrt(z), size)
    p = s * poly(z, ASIN[0])
    p = jnp.where(big, 1.0 - 2.0 * p, p)
    return jnp.where(u < 0.0, -p, p)


def norm_layers(p):
    scales, slopes = [], []
    chain = jnp.ones_like(p)
    for layer in range(LAYERS):
        spread = 1.0 + 2.0 * p
        inv = 1.0 / spread
        scales.append(lax.rsqrt(spread))
        slopes.append(chain * inv)
        if layer < LAYERS - 1:
            chain = chain * (2.0 * TWO_PI) * inv * lax.rsqrt(1.0 + 4.0 * p)
            u = 2.0 * p * inv
            p = scaled_asin(layer, u, u * u)
    return scales, slopes


def ntk_value(g, left, right):
    theta = g
    for layer in range(LAYERS):
        c2 = 2.0 * left[layer] * right[layer]
        u = g * c2
        u2 = u * u
        w = lax.rsqrt(1.0 - u2)
        g = scaled_asin(layer, u, u2)
        theta = g + theta * (TWO_PI * c2 * w)
    return theta


def ntk_full(g, left2, right, slope):
    theta = g
    dg = tg = gr = tr = None
    for layer in range(LAYERS):
        last = layer == LAYERS - 1
        c2 = left2[layer] * right[layer]
        u = g * c2
        u2 = u * u
        w = lax.rsqrt(1.0 - u2)
        cw2 = c2 * w
        step = TWO_PI * cw2
        bend = u * (w * cw2)
        ww = w * w
        tb = theta * bend
        gs = g * slope[layer]
        if layer == 0:
            tg_next = step * (2.0 + tb)
            dg_next = step
            base = -gs
            tr_next = step * (base - theta * (ww * slope[layer]))
        else:
            tg_next = step * (dg + tg + tb * dg)
            dg_next = step * dg
            base = gr - gs
            tr_next = step * (base + tr + (tb * gr - theta * (ww * slope[layer])))
        gr_next = step * base
        g = scaled_asin(layer, u, u2)
        theta = g + step * theta
        tg, dg, gr, tr = tg_next, dg_next, gr_next, tr_next
    return theta, tg, tr


def dot(a, b, dims=NN, precision=None):
    return lax.dot_general(a, b, dims, precision=precision, preferred_element_type=F32)


def split(x):
    high = x.astype(BF16)
    return high, (x - high.astype(F32)).astype(BF16)


def dot3(a, b, dims=NN):
    return dot(a[0], b[0], dims) + (dot(a[0], b[1], dims) + dot(a[1], b[0], dims))


def compute_kernel(
    lab_s, lab_t, sup, tgt,
    grad, slab, inv, system, coef_t, coef_n, own_tg, own_tr,
    gram, gram_ss, kern, tg_s, tr_s, coef, quant, quant_t, left_s, sq, mid, acc,
):
    n_sup = sup.shape[0]
    n_tgt = tgt.shape[0]
    total_tgt = n_tgt * lax.axis_size("sup") * lax.axis_size("tgt")
    own_rows = own_tg.shape[0]

    for j in range(n_sup // 256):
        gram_ss[:, j * 256:(j + 1) * 256] = dot(sup[...], sup[j * 256:(j + 1) * 256, :], NT) * (1.0 / D)

    def gram_tile(j, carry):
        rows = pl.ds(pl.multiple_of(j * 256, 256), 256)
        gram[:, rows] = dot(sup[...], tgt[rows, :], NT) * (1.0 / D)
        return carry

    lax.fori_loop(0, n_tgt // 256, gram_tile, 0)

    def square_tile(j, carry):
        rows = pl.ds(pl.multiple_of(j * 64, 64), 64)
        total = jnp.zeros((64, 128), F32)
        for k in range(D // 128):
            x = tgt[rows, k * 128:(k + 1) * 128].astype(F32)
            total = total + x * x
        sq[rows, :] = total
        return carry

    lax.fori_loop(0, n_tgt // 64, square_tile, 0)
    norm_t = dot(jnp.full((8, 128), 1.0 / D, F32), sq[...], NT, HI)
    scales_t, unused = norm_layers(norm_t)
    for layer in range(LAYERS):
        left_s[layer] = 2.0 * scales_t[layer]
    row_id = lax.broadcasted_iota(jnp.int32, (n_sup, n_sup), 0)
    col_id = lax.broadcasted_iota(jnp.int32, (n_sup, n_sup), 1)
    diagonal = row_id == col_id
    norm_s = jnp.sum(jnp.where(diagonal, gram_ss[...], 0.0), axis=0, keepdims=True)
    scales_s, slopes_s = norm_layers(jnp.broadcast_to(norm_s, (8, n_sup)))
    quant[...] = jnp.zeros_like(quant)
    for layer in range(LAYERS):
        quant[layer * 8:layer * 8 + 8, :] = scales_s[layer]
        quant[64 + layer * 8:72 + layer * 8, :] = slopes_s[layer]
    quant_t[...] = quant[...].T

    def ss_tile(i, carry):
        rows = pl.ds(pl.multiple_of(i * 8, 8), 8)
        q = quant_t[rows, :]
        left = [q[:, l * 8:l * 8 + 1] for l in range(LAYERS)]
        right = [quant[l * 8:l * 8 + 8, :] for l in range(LAYERS)]
        system[rows, :] = ntk_value(gram_ss[rows, :], left, right)
        return carry

    lax.fori_loop(0, n_sup // 8, ss_tile, 0)
    def own_tile(i, carry):
        here = pl.ds(pl.multiple_of(i * 8, 8), 8)
        own = pl.ds(pl.multiple_of(lax.axis_index("sup") * own_rows + i * 8, 8), 8)
        q = quant_t[own, :]
        left = [q[:, l * 8:l * 8 + 1] for l in range(LAYERS)]
        slope = [q[:, 64 + l * 8:65 + l * 8] for l in range(LAYERS)]
        right2 = [2.0 * quant[l * 8:l * 8 + 8, :] for l in range(LAYERS)]
        unused, tg, tr = ntk_full(gram_ss[own, :], right2, left, slope)
        own_tg[here, :] = tg
        own_tr[here, :] = tr
        return carry

    lax.fori_loop(0, own_rows // 8, own_tile, 0)

    half = 512

    def ts_tile(t, carry):
        i, j = t // (n_tgt // half), t % (n_tgt // half)
        rows = pl.ds(pl.multiple_of(i * 8, 8), 8)
        lanes = pl.ds(pl.multiple_of(j * half, half), half)
        q = quant_t[rows, :]
        right = [q[:, l * 8:l * 8 + 1] for l in range(LAYERS)]
        slope = [q[:, 64 + l * 8:65 + l * 8] for l in range(LAYERS)]
        left2 = [left_s[l, :, lanes] for l in range(LAYERS)]
        theta, tg, tr = ntk_full(gram[rows, lanes], left2, right, slope)
        kern[rows, lanes] = theta
        tg_s[rows, lanes] = tg
        tr_s[rows, lanes] = tr
        return carry

    lax.fori_loop(0, (n_sup // 8) * (n_tgt // half), ts_tile, 0)

    kern_ss = system[...]
    trace = jnp.sum(jnp.sum(jnp.where(diagonal, kern_ss, 0.0), axis=0, keepdims=True), axis=1, keepdims=True)
    inv_t = n_sup / trace
    system[...] = kern_ss * inv_t + jnp.where(diagonal, RIDGE, 0.0)
    norms = jnp.sum(jnp.abs(system[...]), axis=0, keepdims=True)
    high = jnp.minimum(jnp.max(norms, axis=1, keepdims=True), n_sup + RIDGE)
    alpha = 2.0 / (high + RIDGE)
    rho = (high - RIDGE) / (high + RIDGE)
    gain = 2.0 / (2.0 - rho * rho)
    inv[...] = (gain * alpha) * (jnp.where(diagonal, 2.0, 0.0) - alpha * system[...])
    rho = 0.5 * gain * rho * rho

    def newton(k, rho):
        a = split(system[...])
        x = split(inv[...])
        mid[...] = jnp.where(diagonal, 2.0, 0.0) - dot3(a, x)
        gain = 2.0 / (2.0 - rho * rho)
        inv[...] = gain * dot3(x, split(mid[...]))
        return 0.5 * gain * rho * rho

    lax.fori_loop(0, NEWTON, newton, rho)
    inv[...] = inv[...] * inv_t
    system[...] = system[...] * (trace * (1.0 / n_sup))

    class_id = lax.broadcasted_iota(jnp.int32, (CLS, n_sup), 0)
    label = jnp.where(class_id == lab_s[...], 1.0, 0.0) - 1.0 / C
    label = jnp.where(class_id < C, label, 0.0)
    coef_t[...] = dot(label, inv[...], NN, HI)
    for k in range(REFINE):
        left_over = label - dot(coef_t[...], system[...], NN, HI)
        coef_t[...] = coef_t[...] + dot(left_over, inv[...], NN, HI)
    coef_n[...] = coef_t[...].T

    class_id = lax.broadcasted_iota(jnp.int32, (CLS, n_tgt), 0)
    label = jnp.where(class_id == lab_t[...], 1.0, 0.0) - 1.0 / C
    label = jnp.where(class_id < C, label, 0.0)
    misfit = dot(coef_t[...], kern[...], NN, HI) - label
    loss = jnp.sum(jnp.sum(misfit * misfit, axis=0, keepdims=True), axis=1, keepdims=True) * (0.5 / total_tgt)
    d_predict = misfit * (1.0 / total_tgt)
    d_coef = dot(kern[...], d_predict, NT, HI)
    gram[...] = dot(coef_n[...], d_predict, NN, HI)

    def pull_tile(i, carry):
        rows = pl.ds(pl.multiple_of(i * 16, 16), 16)
        d_kern = gram[rows, :]
        coef[rows, :] = (d_kern * tg_s[rows, :] * (1.0 / D)).astype(BF16)
        through = d_kern * tr_s[rows, :]
        total = through[:, :128]
        for k in range(1, n_tgt // 128):
            total = total + through[:, k * 128:(k + 1) * 128]
        acc[rows, :] = total
        return carry

    lax.fori_loop(0, n_sup // 16, pull_tile, 0)
    d_norm = jnp.sum(acc[...], axis=1, keepdims=True)
    lane = lax.broadcasted_iota(jnp.int32, (n_sup, CLS), 1)
    d_coef = jnp.where(lane == C, loss, d_coef)
    slab[...] = jnp.where(lane == C + 1, d_norm, d_coef)

    def grad_tile(j, carry):
        lanes = pl.ds(pl.multiple_of(j * 512, 512), 512)
        grad[:, lanes] = dot(coef[...], tgt[:, lanes]).astype(grad.dtype)
        return carry

    lax.fori_loop(0, D // 512, grad_tile, 0)


def compute(gathered, target_images, lab_s, lab_t, own_rows, grad_type):
    n_sup, n_tgt = gathered.shape[0], target_images.shape[0]
    shapes = [
        ((n_sup, D), grad_type), ((n_sup, CLS), F32), ((n_sup, n_sup), F32), ((n_sup, n_sup), F32),
        ((CLS, n_sup), F32), ((n_sup, CLS), F32), ((own_rows, n_sup), F32), ((own_rows, n_sup), F32),
    ]
    vmem = pl.BlockSpec(memory_space=pltpu.VMEM)
    return pl.pallas_call(
        compute_kernel,
        out_shape=[jax.ShapeDtypeStruct(s, t) for s, t in shapes],
        in_specs=[vmem] * 4,
        out_specs=[vmem] * len(shapes),
        scratch_shapes=[
            pltpu.VMEM((n_sup, n_tgt), F32), pltpu.VMEM((n_sup, n_sup), F32),
            pltpu.VMEM((n_sup, n_tgt), F32), pltpu.VMEM((n_sup, n_tgt), F32), pltpu.VMEM((n_sup, n_tgt), F32),
            pltpu.VMEM((n_sup, n_tgt), BF16),
            pltpu.VMEM((128, n_sup), F32), pltpu.VMEM((n_sup, 128), F32),
            pltpu.VMEM((LAYERS, 8, n_tgt), F32), pltpu.VMEM((n_tgt, 128), F32),
            pltpu.VMEM((n_sup, n_sup), F32), pltpu.VMEM((n_sup, 128), F32),
        ],
        compiler_params=pltpu.CompilerParams(vmem_limit_bytes=56 * 2**20),
        name="compute",
    )(lab_s, lab_t, gathered, target_images)


def finish_kernel(sup, grad_own, total, inv, system, coef_t, coef_n, own_tg, own_tr, out, loss):
    n_sup = sup.shape[0]
    own_rows = grad_own.shape[0]
    start = pl.multiple_of(lax.axis_index("sup") * own_rows, 8)
    own = pl.ds(start, own_rows)
    lane = lax.broadcasted_iota(jnp.int32, (n_sup, CLS), 1)
    d_coef = jnp.where(lane < C, total[...], 0.0)
    adjoint = dot(inv[...], d_coef, NN, HI)
    for k in range(REFINE):
        left_over = d_coef - dot(system[...], adjoint, NN, HI)
        adjoint = adjoint + dot(inv[...], left_over, NN, HI)
    coefs = coef_n[...]
    ridge = jnp.sum(jnp.sum(adjoint * coefs, axis=0, keepdims=True), axis=1, keepdims=True) * (-RIDGE / n_sup)
    row_id = lax.broadcasted_iota(jnp.int32, (own_rows, n_sup), 0) + start
    col_id = lax.broadcasted_iota(jnp.int32, (own_rows, n_sup), 1)
    mine = row_id == col_id
    pick = jnp.where(mine, 1.0, 0.0)
    adj_own = dot(pick, adjoint, NN, HI)
    d_kern = jnp.where(mine, 2.0 * ridge, 0.0) - dot(adj_own, coef_t[...], NN, HI)
    d_kern = d_kern - dot(coef_n[own, :], adjoint, NT, HI)
    weight = d_kern * own_tg[...] * (1.0 / D)
    lane = lax.broadcasted_iota(jnp.int32, (own_rows, CLS), 1)
    slab_own = total[own, :]
    d_norm = jnp.sum(d_kern * own_tr[...], axis=1, keepdims=True)
    d_norm = d_norm + jnp.sum(jnp.where(lane == C + 1, slab_own, 0.0), axis=1, keepdims=True)
    loss[...] = jnp.where(lane == C, slab_own, 0.0)
    high, low = split(weight)
    for k in range(D // 512):
        lanes = slice(k * 512, (k + 1) * 512)
        part = dot(high, sup[:, lanes]) + dot(low, sup[:, lanes])
        part = part + grad_own[:, lanes].astype(F32)
        part = part + (2.0 / D) * d_norm * sup[own, lanes].astype(F32)
        out[:, lanes] = n_sup * part


def finish(gathered, grad_own, total, inv, system, coef_t, coef_n, own_tg, own_tr):
    own_rows = grad_own.shape[0]
    vmem = pl.BlockSpec(memory_space=pltpu.VMEM)
    return pl.pallas_call(
        finish_kernel,
        out_shape=[jax.ShapeDtypeStruct((own_rows, D), F32), jax.ShapeDtypeStruct((own_rows, CLS), F32)],
        in_specs=[vmem] * 9,
        out_specs=[vmem] * 2,
        compiler_params=pltpu.CompilerParams(vmem_limit_bytes=48 * 2**20),
        name="finish",
    )(gathered, grad_own, total, inv, system, coef_t, coef_n, own_tg, own_tr)


def body(support_images, target_images, support_labels, target_labels):
    own_rows = support_images.shape[0]
    lab_s = support_labels.reshape(1, -1)
    lab_t = target_labels.reshape(1, -1)
    gathered = lax.all_gather(support_images, "sup", axis=0, tiled=True)
    grad, slab, *rest = compute(gathered, target_images, lab_s, lab_t, own_rows, F32)
    total = lax.psum(slab, ("tgt", "sup"))
    grad_own = lax.psum(lax.psum_scatter(grad, "sup", scatter_dimension=0, tiled=True), "tgt")
    out, loss = finish(gathered, grad_own, total, *rest)
    return out, jnp.sum(loss[0])


def solution(mesh):
    in_specs = (P("sup", None), P(("tgt", "sup"), None), P(), P(("tgt", "sup")))
    out_specs = (P("sup", None), P())
    return jax.shard_map(body, mesh=mesh, in_specs=in_specs, out_specs=out_specs, check_vma=False)
```

```python
import functools
import math

import jax
import jax.numpy as jnp
from jax import lax
from jax.experimental import pallas as pl
from jax.experimental.pallas import tpu as pltpu
from jax.sharding import PartitionSpec as P

D = 3072
C = 100
LAYERS = 5
CLS = 128
RIDGE = 0.1
TWO_PI = 2.0 / math.pi
NEWTON = 7
REFINE = 3
HI = lax.Precision.HIGHEST
NN = (((1,), (0,)), ((), ()))
NT = (((1,), (1,)), ((), ()))
F32 = jnp.float32
BF16 = jnp.bfloat16

ASIN = (
    (1.0, 0.1666678637266159, 0.0749453455209732, 0.0455390103161335, 0.02390936389565468, 0.042553599923849106),
    (1.0, 0.16666781902313232, 0.07494797557592392, 0.04552660509943962, 0.02313542366027832, 0.0537058524787426, -0.05348314717411995, 0.08573318272829056),
    (1.0, 0.16666752099990845, 0.07495901733636856, 0.04535885155200958, 0.024863531813025475, 0.04080614075064659),
    (1.0, 0.16666492819786072, 0.0750882476568222, 0.043096426874399185, 0.04107564687728882),
    (1.0, 0.16666613519191742, 0.07503537833690643, 0.043817341327667236, 0.03804752230644226),
)


def poly(z, coefs):
    total = coefs[-1] * TWO_PI
    for value in coefs[-2::-1]:
        total = total * z + value * TWO_PI
    return total


def scaled_asin(layer, u, u2):
    if layer > 0:
        return u * poly(u2, ASIN[layer])
    size = jnp.abs(u)
    big = size > 0.5
    z = jnp.where(big, 0.5 - 0.5 * size, u2)
    s = jnp.where(big, z * lax.rsqrt(z), size)
    p = s * poly(z, ASIN[0])
    p = jnp.where(big, 1.0 - 2.0 * p, p)
    return jnp.where(u < 0.0, -p, p)


def norm_layers(p):
    scales, slopes = [], []
    chain = jnp.ones_like(p)
    for layer in range(LAYERS):
        spread = 1.0 + 2.0 * p
        inv = 1.0 / spread
        scales.append(lax.rsqrt(spread))
        slopes.append(chain * inv)
        if layer < LAYERS - 1:
            chain = chain * (2.0 * TWO_PI) * inv * lax.rsqrt(1.0 + 4.0 * p)
            u = 2.0 * p * inv
            p = scaled_asin(layer, u, u * u)
    return scales, slopes


def ntk_value(g, left, right):
    theta = g
    for layer in range(LAYERS):
        c2 = 2.0 * left[layer] * right[layer]
        u = g * c2
        u2 = u * u
        w = lax.rsqrt(1.0 - u2)
        g = scaled_asin(layer, u, u2)
        theta = g + theta * (TWO_PI * c2 * w)
    return theta


def ntk_full(g, left2, right, slope):
    theta = g
    dg = tg = gr = tr = None
    for layer in range(LAYERS):
        last = layer == LAYERS - 1
        c2 = left2[layer] * right[layer]
        u = g * c2
        u2 = u * u
        w = lax.rsqrt(1.0 - u2)
        cw2 = c2 * w
        step = TWO_PI * cw2
        bend = u * (w * cw2)
        ww = w * w
        tb = theta * bend
        gs = g * slope[layer]
        if layer == 0:
            tg_next = step * (2.0 + tb)
            dg_next = step
            base = -gs
            tr_next = step * (base - theta * (ww * slope[layer]))
        else:
            tg_next = step * (dg + tg + tb * dg)
            dg_next = step * dg
            base = gr - gs
            tr_next = step * (base + tr + (tb * gr - theta * (ww * slope[layer])))
        gr_next = step * base
        g = scaled_asin(layer, u, u2)
        theta = g + step * theta
        tg, dg, gr, tr = tg_next, dg_next, gr_next, tr_next
    return theta, tg, tr


def dot(a, b, dims=NN, precision=None):
    return lax.dot_general(a, b, dims, precision=precision, preferred_element_type=F32)


def split(x):
    high = x.astype(BF16)
    return high, (x - high.astype(F32)).astype(BF16)


def dot3(a, b, dims=NN):
    return dot(a[0], b[0], dims) + (dot(a[0], b[1], dims) + dot(a[1], b[0], dims))


def load_images(gathered, sup, sems):
    half = D // 2
    copies = []
    for y in range(4):
        for x in range(4):
            rows = pl.ds(32 * (y * 4 + x), 32)
            for h, slot in ((0, y * 4 + x), (1, x * 4 + y)):
                dst = sup.at[rows, h * half:(h + 1) * half]
                copies.append(pltpu.make_async_copy(gathered.at[h, slot], dst, sems.at[len(copies)]))
    for copy in copies:
        copy.start()
    return copies


def compute_kernel(
    lab_s, lab_t, gathered, tgt,
    grad, slab, inv, system, coef_t, coef_n, own_tg, own_tr,
    sup, gram, gram_ss, kern, tg_s, tr_s, coef, quant, quant_t, left_s, sq, mid, acc, sems,
):
    for copy in load_images(gathered, sup, sems):
        copy.wait()
    n_sup = sup.shape[0]
    n_tgt = tgt.shape[0]
    total_tgt = n_tgt * lax.axis_size("sup") * lax.axis_size("tgt")
    own_rows = own_tg.shape[0]

    for j in range(n_sup // 256):
        gram_ss[:, j * 256:(j + 1) * 256] = dot(sup[...], sup[j * 256:(j + 1) * 256, :], NT) * (1.0 / D)

    def gram_tile(j, carry):
        rows = pl.ds(pl.multiple_of(j * 256, 256), 256)
        gram[:, rows] = dot(sup[...], tgt[rows, :], NT) * (1.0 / D)
        return carry

    lax.fori_loop(0, n_tgt // 256, gram_tile, 0)

    def square_tile(j, carry):
        rows = pl.ds(pl.multiple_of(j * 64, 64), 64)
        total = jnp.zeros((64, 128), F32)
        for k in range(D // 128):
            x = tgt[rows, k * 128:(k + 1) * 128].astype(F32)
            total = total + x * x
        sq[rows, :] = total
        return carry

    lax.fori_loop(0, n_tgt // 64, square_tile, 0)
    norm_t = dot(jnp.full((8, 128), 1.0 / D, F32), sq[...], NT, HI)
    scales_t, unused = norm_layers(norm_t)
    for layer in range(LAYERS):
        left_s[layer] = 2.0 * scales_t[layer]
    row_id = lax.broadcasted_iota(jnp.int32, (n_sup, n_sup), 0)
    col_id = lax.broadcasted_iota(jnp.int32, (n_sup, n_sup), 1)
    diagonal = row_id == col_id
    norm_s = jnp.sum(jnp.where(diagonal, gram_ss[...], 0.0), axis=0, keepdims=True)
    scales_s, slopes_s = norm_layers(jnp.broadcast_to(norm_s, (8, n_sup)))
    quant[...] = jnp.zeros_like(quant)
    for layer in range(LAYERS):
        quant[layer * 8:layer * 8 + 8, :] = scales_s[layer]
        quant[64 + layer * 8:72 + layer * 8, :] = slopes_s[layer]
    quant_t[...] = quant[...].T

    def ss_tile(i, carry):
        rows = pl.ds(pl.multiple_of(i * 8, 8), 8)
        q = quant_t[rows, :]
        left = [q[:, l * 8:l * 8 + 1] for l in range(LAYERS)]
        right = [quant[l * 8:l * 8 + 8, :] for l in range(LAYERS)]
        system[rows, :] = ntk_value(gram_ss[rows, :], left, right)
        return carry

    lax.fori_loop(0, n_sup // 8, ss_tile, 0)
    def own_tile(i, carry):
        here = pl.ds(pl.multiple_of(i * 8, 8), 8)
        own = pl.ds(pl.multiple_of(lax.axis_index("sup") * own_rows + i * 8, 8), 8)
        q = quant_t[own, :]
        left = [q[:, l * 8:l * 8 + 1] for l in range(LAYERS)]
        slope = [q[:, 64 + l * 8:65 + l * 8] for l in range(LAYERS)]
        right2 = [2.0 * quant[l * 8:l * 8 + 8, :] for l in range(LAYERS)]
        unused, tg, tr = ntk_full(gram_ss[own, :], right2, left, slope)
        own_tg[here, :] = tg
        own_tr[here, :] = tr
        return carry

    lax.fori_loop(0, own_rows // 8, own_tile, 0)

    half = 512

    def ts_tile(t, carry):
        i, j = t // (n_tgt // half), t % (n_tgt // half)
        rows = pl.ds(pl.multiple_of(i * 8, 8), 8)
        lanes = pl.ds(pl.multiple_of(j * half, half), half)
        q = quant_t[rows, :]
        right = [q[:, l * 8:l * 8 + 1] for l in range(LAYERS)]
        slope = [q[:, 64 + l * 8:65 + l * 8] for l in range(LAYERS)]
        left2 = [left_s[l, :, lanes] for l in range(LAYERS)]
        theta, tg, tr = ntk_full(gram[rows, lanes], left2, right, slope)
        kern[rows, lanes] = theta
        tg_s[rows, lanes] = tg
        tr_s[rows, lanes] = tr
        return carry

    lax.fori_loop(0, (n_sup // 8) * (n_tgt // half), ts_tile, 0)

    kern_ss = system[...]
    trace = jnp.sum(jnp.sum(jnp.where(diagonal, kern_ss, 0.0), axis=0, keepdims=True), axis=1, keepdims=True)
    inv_t = n_sup / trace
    system[...] = kern_ss * inv_t + jnp.where(diagonal, RIDGE, 0.0)
    norms = jnp.sum(jnp.abs(system[...]), axis=0, keepdims=True)
    high = jnp.minimum(jnp.max(norms, axis=1, keepdims=True), n_sup + RIDGE)
    alpha = 2.0 / (high + RIDGE)
    rho = (high - RIDGE) / (high + RIDGE)
    gain = 2.0 / (2.0 - rho * rho)
    inv[...] = (gain * alpha) * (jnp.where(diagonal, 2.0, 0.0) - alpha * system[...])
    rho = 0.5 * gain * rho * rho

    def newton(k, rho):
        a = split(system[...])
        x = split(inv[...])
        mid[...] = jnp.where(diagonal, 2.0, 0.0) - dot3(a, x)
        gain = 2.0 / (2.0 - rho * rho)
        inv[...] = gain * dot3(x, split(mid[...]))
        return 0.5 * gain * rho * rho

    lax.fori_loop(0, NEWTON, newton, rho)
    inv[...] = inv[...] * inv_t
    system[...] = system[...] * (trace * (1.0 / n_sup))

    class_id = lax.broadcasted_iota(jnp.int32, (CLS, n_sup), 0)
    label = jnp.where(class_id == lab_s[...], 1.0, 0.0) - 1.0 / C
    label = jnp.where(class_id < C, label, 0.0)
    coef_t[...] = dot(label, inv[...], NN, HI)
    for k in range(REFINE):
        left_over = label - dot(coef_t[...], system[...], NN, HI)
        coef_t[...] = coef_t[...] + dot(left_over, inv[...], NN, HI)
    coef_n[...] = coef_t[...].T

    class_id = lax.broadcasted_iota(jnp.int32, (CLS, n_tgt), 0)
    label = jnp.where(class_id == lab_t[...], 1.0, 0.0) - 1.0 / C
    label = jnp.where(class_id < C, label, 0.0)
    misfit = dot(coef_t[...], kern[...], NN, HI) - label
    loss = jnp.sum(jnp.sum(misfit * misfit, axis=0, keepdims=True), axis=1, keepdims=True) * (0.5 / total_tgt)
    d_predict = misfit * (1.0 / total_tgt)
    d_coef = dot(kern[...], d_predict, NT, HI)
    gram[...] = dot(coef_n[...], d_predict, NN, HI)

    def pull_tile(i, carry):
        rows = pl.ds(pl.multiple_of(i * 16, 16), 16)
        d_kern = gram[rows, :]
        part = (d_kern * tg_s[rows, :] * (1.0 / D)).astype(BF16)
        coef[0, rows, :] = part
        block = i // 2
        other = (block % 4) * 4 + block // 4
        coef[1, pl.ds(pl.multiple_of(other * 32 + (i % 2) * 16, 16), 16), :] = part
        through = d_kern * tr_s[rows, :]
        total = through[:, :128]
        for k in range(1, n_tgt // 128):
            total = total + through[:, k * 128:(k + 1) * 128]
        acc[rows, :] = total
        return carry

    lax.fori_loop(0, n_sup // 16, pull_tile, 0)
    d_norm = jnp.sum(acc[...], axis=1, keepdims=True)
    lane = lax.broadcasted_iota(jnp.int32, (n_sup, CLS), 1)
    d_coef = jnp.where(lane == C, loss, d_coef)
    acc[...] = jnp.where(lane == C + 1, d_norm, d_coef)
    slab[0] = acc[...]
    for y in range(4):
        for x in range(4):
            slab[1, 32 * (x * 4 + y):32 * (x * 4 + y) + 32, :] = acc[32 * (y * 4 + x):32 * (y * 4 + x) + 32, :]

    for h in range(2):
        def grad_tile(j, carry):
            there = pl.ds(pl.multiple_of(j * 512, 512), 512)
            lanes = pl.ds(pl.multiple_of(j * 512 + h * (D // 2), 512), 512)
            grad[h, :, there] = dot(coef[h], tgt[:, lanes]).astype(grad.dtype)
            return carry

        lax.fori_loop(0, D // 1024, grad_tile, 0)


def compute(gathered, target_images, lab_s, lab_t, own_rows):
    n_sup, n_tgt = gathered.size // D, target_images.shape[0]
    shapes = [
        ((2, n_sup, D // 2), BF16), ((2, n_sup, CLS), F32), ((n_sup, n_sup), F32), ((n_sup, n_sup), F32),
        ((CLS, n_sup), F32), ((n_sup, CLS), F32), ((own_rows, n_sup), F32), ((own_rows, n_sup), F32),
    ]
    vmem = pl.BlockSpec(memory_space=pltpu.VMEM)
    return pl.pallas_call(
        compute_kernel,
        out_shape=[jax.ShapeDtypeStruct(s, t) for s, t in shapes],
        in_specs=[vmem, vmem, pl.BlockSpec(memory_space=pl.ANY), vmem],
        out_specs=[vmem] * len(shapes),
        scratch_shapes=[
            pltpu.VMEM((n_sup, D), BF16),
            pltpu.VMEM((n_sup, n_tgt), F32), pltpu.VMEM((n_sup, n_sup), F32),
            pltpu.VMEM((n_sup, n_tgt), F32), pltpu.VMEM((n_sup, n_tgt), F32), pltpu.VMEM((n_sup, n_tgt), F32),
            pltpu.VMEM((2, n_sup, n_tgt), BF16),
            pltpu.VMEM((128, n_sup), F32), pltpu.VMEM((n_sup, 128), F32),
            pltpu.VMEM((LAYERS, 8, n_tgt), F32), pltpu.VMEM((n_tgt, 128), F32),
            pltpu.VMEM((n_sup, n_sup), F32), pltpu.VMEM((n_sup, 128), F32),
            pltpu.SemaphoreType.DMA((32,)),
        ],
        compiler_params=pltpu.CompilerParams(vmem_limit_bytes=56 * 2**20),
        name="compute",
    )(lab_s, lab_t, gathered, target_images)


def finish_kernel(gathered, images, grad_own, total, inv, system, coef_t, coef_n, own_tg, own_tr, out, loss, sup, sems):
    copies = load_images(gathered, sup, sems)
    n_sup = sup.shape[0]
    own_rows = grad_own.shape[1]
    start = pl.multiple_of(lax.axis_index("sup") * own_rows, 8)
    own = pl.ds(start, own_rows)
    lane = lax.broadcasted_iota(jnp.int32, (n_sup, CLS), 1)
    d_coef = jnp.where(lane < C, total[...], 0.0)
    adjoint = dot(inv[...], d_coef, NN, HI)
    for k in range(REFINE):
        left_over = d_coef - dot(system[...], adjoint, NN, HI)
        adjoint = adjoint + dot(inv[...], left_over, NN, HI)
    coefs = coef_n[...]
    ridge = jnp.sum(jnp.sum(adjoint * coefs, axis=0, keepdims=True), axis=1, keepdims=True) * (-RIDGE / n_sup)
    row_id = lax.broadcasted_iota(jnp.int32, (own_rows, n_sup), 0) + start
    col_id = lax.broadcasted_iota(jnp.int32, (own_rows, n_sup), 1)
    mine = row_id == col_id
    pick = jnp.where(mine, 1.0, 0.0)
    adj_own = dot(pick, adjoint, NN, HI)
    d_kern = jnp.where(mine, 2.0 * ridge, 0.0) - dot(adj_own, coef_t[...], NN, HI)
    d_kern = d_kern - dot(coef_n[own, :], adjoint, NT, HI)
    weight = d_kern * own_tg[...] * (1.0 / D)
    lane = lax.broadcasted_iota(jnp.int32, (own_rows, CLS), 1)
    slab_own = total[own, :]
    d_norm = jnp.sum(d_kern * own_tr[...], axis=1, keepdims=True)
    d_norm = d_norm + jnp.sum(jnp.where(lane == C + 1, slab_own, 0.0), axis=1, keepdims=True)
    loss[...] = jnp.where(lane == C, total[:own_rows, :], 0.0)
    high, low = split(weight)
    for copy in copies:
        copy.wait()
    for k in range(D // 512):
        lanes = slice(k * 512, (k + 1) * 512)
        part = dot(high, sup[:, lanes]) + dot(low, sup[:, lanes])
        h, shift = divmod(k, D // 1024)
        part = part + grad_own[h, :, shift * 512:(shift + 1) * 512]
        part = part + (2.0 / D) * d_norm * images[:, lanes].astype(F32)
        out[:, lanes] = n_sup * part


def finish(gathered, images, grad_own, total, inv, system, coef_t, coef_n, own_tg, own_tr):
    own_rows = grad_own.shape[1]
    vmem = pl.BlockSpec(memory_space=pltpu.VMEM)
    return pl.pallas_call(
        finish_kernel,
        out_shape=[jax.ShapeDtypeStruct((own_rows, D), F32), jax.ShapeDtypeStruct((own_rows, CLS), F32)],
        in_specs=[pl.BlockSpec(memory_space=pl.ANY)] + [vmem] * 9,
        out_specs=[vmem] * 2,
        scratch_shapes=[pltpu.VMEM((inv.shape[0], D), BF16), pltpu.SemaphoreType.DMA((32,))],
        compiler_params=pltpu.CompilerParams(vmem_limit_bytes=48 * 2**20),
        name="finish",
    )(gathered, images, grad_own, total, inv, system, coef_t, coef_n, own_tg, own_tr)


MESH = pl.DeviceIdType.MESH
RING = 4


def place():
    tgt, sup = lax.axis_index("tgt"), lax.axis_index("sup")
    core = tgt % 2
    zh = sup % RING
    x = (sup // RING) % RING
    y = sup // (RING * RING)
    a = y + core * (x - y)
    b = x + core * (y - x)
    step_a, step_b = RING - (RING - 1) * core, 1 + (RING - 1) * core

    def device(a_there, b_there, zh_there):
        return (tgt, (a_there * step_a + b_there * step_b) * RING + zh_there)

    partner = (tgt + 1 - 2 * core, sup)
    beside = ((tgt + 2) % 4, sup)
    return core, y, x, a, b, zh, device, partner, beside


def turn(index, by):
    return (index + by) % RING


def greet(devices):
    barrier = pltpu.get_barrier_semaphore()
    for device in devices:
        pl.semaphore_signal(barrier, inc=1, device_id=device, device_id_type=MESH)
    pl.semaphore_wait(barrier, len(devices))


class Sender:
    def __init__(self, send_sems, recv_sems):
        self.send_sems, self.recv_sems, self.made = send_sems, recv_sems, []

    def start(self, src, dst, device):
        k = len(self.made)
        copy = pltpu.make_async_remote_copy(
            src_ref=src, dst_ref=dst, send_sem=self.send_sems.at[k], recv_sem=self.recv_sems.at[k],
            device_id=device, device_id_type=MESH)
        copy.start()
        self.made.append(copy)
        return copy

    def drain(self):
        for copy in self.made:
            copy.wait_send()


def ring_gather(sender, block, me, left, right, then=None):
    then = then or (lambda ref: None)
    low, high = pl.ds(0, 2), pl.ds(2, 2)
    to_right = sender.start(block(me), block(me), right)
    to_left = sender.start(block(me), block(me), left)
    to_right.wait_recv()
    before = block(turn(me, 3))
    far_right = sender.start(before.at[low], before.at[low], right)
    to_left.wait_recv()
    after = block(turn(me, 1))
    far_left = sender.start(after.at[high], after.at[high], left)
    then(before)
    then(after)
    far = block(turn(me, 2))
    far_right.wait_recv()
    then(far.at[low])
    far_left.wait_recv()
    then(far.at[high])


def gather_kernel(own, out, send_sems, recv_sems, local_sem):
    core, y, x, a, b, zh, device, partner, beside = place()
    greet(
        [device(a, b, turn(zh, k)) for k in (1, 2, 3)]
        + [device(a, turn(b, k), zh) for k in (1, 3)] + [device(turn(a, k), b, zh) for k in (1, 3)] + [partner]
    )
    half = out.shape[-1]
    mine = own.at[:, pl.ds(pl.multiple_of(core * half, 128), half)]
    sender = Sender(send_sems, recv_sems)
    first = [sender.start(mine, out.at[core, a, b, zh], device(a, b, turn(zh, k))) for k in (1, 3, 2)]
    local = pltpu.make_async_copy(mine, out.at[core, a, b, zh], local_sem)
    local.start()
    local.wait()
    for copy in first:
        copy.wait_recv()
    ring_gather(sender, lambda i: out.at[core, a, i], b, device(a, turn(b, 3), zh), device(a, turn(b, 1), zh))
    across = []

    def share(ref):
        across.append(sender.start(ref, ref, partner))

    share(out.at[core, a])
    ring_gather(sender, lambda i: out.at[core, i], a, device(turn(a, 3), b, zh), device(turn(a, 1), b, zh), share)
    for copy in across:
        copy.wait_recv()
    sender.drain()


def gather_images(support_images):
    rows = support_images.shape[0]
    return pl.pallas_call(
        gather_kernel,
        out_shape=jax.ShapeDtypeStruct((2, RING, RING, RING, rows, D // 2), BF16),
        in_specs=[pl.BlockSpec(memory_space=pl.ANY)],
        out_specs=pl.BlockSpec(memory_space=pl.ANY),
        scratch_shapes=[pltpu.SemaphoreType.DMA((16,)), pltpu.SemaphoreType.DMA((16,)), pltpu.SemaphoreType.DMA],
        compiler_params=pltpu.CompilerParams(collective_id=0, has_side_effects=True),
        name="gather",
    )(support_images)


def add_blocks(dst, parts, lead):
    count = math.prod(lead)

    def one(t, carry):
        index = []
        for length in reversed(lead):
            index.append(t % length)
            t = t // length
        index = tuple(reversed(index))
        total = dst[index].astype(F32)
        for part in parts:
            total = total + part[index].astype(F32)
        dst[index] = total.astype(dst.dtype)
        return carry

    lax.fori_loop(0, count, one, 0)


class Scatter:
    def __init__(self, source, work, near_a, far_a, near_b, far_b, tail, near_z, ends, sender):
        self.source, self.work, self.near_a, self.far_a = source, work, near_a, far_a
        self.near_b, self.far_b, self.tail, self.near_z = near_b, far_b, tail, near_z
        self.ends, self.sender = ends, sender


def ring_scatter_start(array, near, block, me, left, right):
    far = block(turn(me, 2))
    to_right = array.sender.start(far.at[pl.ds(0, 2)], near.at[0], right)
    to_left = array.sender.start(far.at[pl.ds(2, 2)], near.at[1], left)
    return to_right, to_left


def ring_scatter_middle(array, near, landing, block, me, left, right, copies, lead):
    to_right, to_left = copies
    after, before = block(turn(me, 1)), block(turn(me, 3))
    to_right.wait_recv()
    add_blocks(after.at[pl.ds(0, 2)], [near.at[0]], (2,) + lead)
    second_right = array.sender.start(after, landing.at[0], right)
    to_left.wait_recv()
    add_blocks(before.at[pl.ds(2, 2)], [near.at[1]], (2,) + lead)
    second_left = array.sender.start(before, landing.at[1], left)
    return second_right, second_left


def scatter_kernel(grad, slab, out_grad, out_slab, *scratch):
    core, y, x, a, b, zh, device, partner, beside = place()
    greet(
        [device(a, b, turn(zh, k)) for k in (1, 2, 3)]
        + [device(a, turn(b, k), zh) for k in (1, 3)] + [device(turn(a, k), b, zh) for k in (1, 3)] + [partner, beside]
    )
    sems = scratch[-4:]
    arrays = [
        Scatter(slab, *scratch[8:16], Sender(sems[2], sems[3])),
        Scatter(grad, *scratch[0:8], Sender(sems[0], sems[1])),
    ]
    left_a, right_a = device(turn(a, 3), b, zh), device(turn(a, 1), b, zh)
    left_b, right_b = device(a, turn(b, 3), zh), device(a, turn(b, 1), zh)
    order = (2, 1, 3, 0)
    pair = {}
    for k in order:
        for n, array in enumerate(arrays):
            there = turn(b, k)
            pair[n, k] = array.sender.start(array.source.at[1 - core, there], array.work.at[there], partner)
    first, second = {}, {}
    for k in order:
        for n, array in enumerate(arrays):
            pair[n, k].wait_recv()
            here = turn(a, k)
            add_blocks(array.work.at[here], [array.source.at[core, here]], (RING, RING))
            if k == 2:
                first[n] = ring_scatter_start(array, array.near_a, lambda i: array.work.at[i], a, left_a, right_a)
        if k == 3:
            for n, array in enumerate(arrays):
                second[n] = ring_scatter_middle(
                    array, array.near_a, array.far_a, lambda i: array.work.at[i], a, left_a, right_a, first[n], (RING,))
    for n, array in enumerate(arrays):
        for copy in second[n]:
            copy.wait_recv()
        add_blocks(array.work.at[a], [array.far_a.at[0], array.far_a.at[1]], (RING, RING))
        first[n] = ring_scatter_start(array, array.near_b, lambda i: array.work.at[a, i], b, left_b, right_b)
    for n, array in enumerate(arrays):
        second[n] = ring_scatter_middle(
            array, array.near_b, array.far_b, lambda i: array.work.at[a, i], b, left_b, right_b, first[n], ())
    third = {}
    for n, array in enumerate(arrays):
        for copy in second[n]:
            copy.wait_recv()
        for i in range(RING):
            array.tail[i] = (
                array.work[a, b, i].astype(F32) + array.far_b[0, i].astype(F32) + array.far_b[1, i].astype(F32))
        third[n] = [
            array.sender.start(array.tail.at[turn(zh, k)], array.near_z.at[k - 1], device(a, b, turn(zh, k)))
            for k in (2, 1, 3)]
    fourth = {}
    for n, array in enumerate(arrays):
        for copy in third[n]:
            copy.wait_recv()
        array.ends[0] = array.tail[zh] + array.near_z[0] + (array.near_z[1] + array.near_z[2])
        fourth[n] = array.sender.start(array.ends.at[0], array.ends.at[1], beside)
    slab_a, grad_a = arrays
    fourth[0].wait_recv()
    slab_a.ends[2] = slab_a.ends[0] + slab_a.ends[1]
    swap = slab_a.sender.start(slab_a.ends.at[2], slab_a.ends.at[3], partner)
    fourth[1].wait_recv()
    out_grad[core] = grad_a.ends[0] + grad_a.ends[1]
    last = grad_a.sender.start(out_grad.at[core], out_grad.at[core], partner)
    swap.wait_recv()
    out_slab[y, x, zh] = jnp.where(core == 0, slab_a.ends[2], slab_a.ends[3])
    sender = slab_a.sender
    spot = out_slab.at[y, x, zh]
    ring_z = [sender.start(spot, spot, device(a, b, turn(zh, k))) for k in (2, 1, 3)]
    for copy in ring_z:
        copy.wait_recv()

    def at_x(k):
        return (lax.axis_index("tgt"), (y * RING + turn(x, k)) * RING + zh)

    def at_y(k):
        return (lax.axis_index("tgt"), (turn(y, k) * RING + x) * RING + zh)

    ring_gather(sender, lambda i: out_slab.at[y, i], x, at_x(3), at_x(1))
    ring_gather(sender, lambda i: out_slab.at[i], y, at_y(3), at_y(1))
    last.wait_recv()
    for array in arrays:
        array.sender.drain()


def scatter_sums(grad, slab, rows):
    def buffers(lanes, dtype):
        return [
            pltpu.VMEM((RING, RING, RING, rows, lanes), dtype),
            pltpu.VMEM((2, 2, RING, rows, lanes), dtype),
            pltpu.VMEM((2, RING, RING, rows, lanes), dtype),
            pltpu.VMEM((2, 2, rows, lanes), dtype),
            pltpu.VMEM((2, RING, rows, lanes), dtype),
            pltpu.VMEM((RING, rows, lanes), F32),
            pltpu.VMEM((3, rows, lanes), F32),
            pltpu.VMEM((4, rows, lanes), F32),
        ]

    vmem = pl.BlockSpec(memory_space=pltpu.VMEM)
    half = D // 2
    return pl.pallas_call(
        scatter_kernel,
        out_shape=[
            jax.ShapeDtypeStruct((2, rows, half), F32),
            jax.ShapeDtypeStruct((RING, RING, RING, rows, CLS), F32),
        ],
        in_specs=[vmem] * 2,
        out_specs=[vmem] * 2,
        scratch_shapes=buffers(half, BF16) + buffers(CLS, F32) + [
            pltpu.SemaphoreType.DMA((20,)), pltpu.SemaphoreType.DMA((20,)),
            pltpu.SemaphoreType.DMA((32,)), pltpu.SemaphoreType.DMA((32,)),
        ],
        compiler_params=pltpu.CompilerParams(
            collective_id=1, has_side_effects=True, vmem_limit_bytes=40 * 2**20),
        name="scatter",
    )(grad.reshape(2, RING, RING, RING, rows, half), slab.reshape(2, RING, RING, RING, rows, CLS))


def body(support_images, target_images, support_labels, target_labels):
    own_rows = support_images.shape[0]
    lab_s = support_labels.reshape(1, -1)
    lab_t = target_labels.reshape(1, -1)
    gathered = gather_images(support_images).reshape(2, RING * RING, RING * own_rows, D // 2)
    grad, slab, *rest = compute(gathered, target_images, lab_s, lab_t, own_rows)
    grad_own, total = scatter_sums(grad, slab, own_rows)
    out, loss = finish(gathered, support_images, grad_own, total.reshape(-1, CLS), *rest)
    return out, jnp.sum(loss[0])


def solution(mesh):
    in_specs = (P("sup", None), P(("tgt", "sup"), None), P(), P(("tgt", "sup")))
    out_specs = (P("sup", None), P())
    return jax.shard_map(body, mesh=mesh, in_specs=in_specs, out_specs=out_specs, check_vma=False)
```

```python
import functools
import math

import jax
import jax.numpy as jnp
from jax import lax
from jax.experimental import pallas as pl
from jax.experimental.pallas import tpu as pltpu
from jax.sharding import PartitionSpec as P

D = 3072
C = 100
LAYERS = 5
CLS = 128
RIDGE = 0.1
TWO_PI = 2.0 / math.pi
NEWTON = 7
REFINE = 2
HI = lax.Precision.HIGHEST
NN = (((1,), (0,)), ((), ()))
NT = (((1,), (1,)), ((), ()))
F32 = jnp.float32
BF16 = jnp.bfloat16

ASIN = (
    (1.0, 0.1666678637266159, 0.0749453455209732, 0.0455390103161335, 0.02390936389565468, 0.042553599923849106),
    (1.0, 0.16666781902313232, 0.07494797557592392, 0.04552660509943962, 0.02313542366027832, 0.0537058524787426, -0.05348314717411995, 0.08573318272829056),
    (1.0, 0.16666752099990845, 0.07495901733636856, 0.04535885155200958, 0.024863531813025475, 0.04080614075064659),
    (1.0, 0.16666492819786072, 0.0750882476568222, 0.043096426874399185, 0.04107564687728882),
    (1.0, 0.16666613519191742, 0.07503537833690643, 0.043817341327667236, 0.03804752230644226),
)


def poly(z, coefs):
    total = coefs[-1] * TWO_PI
    for value in coefs[-2::-1]:
        total = total * z + value * TWO_PI
    return total


def scaled_asin(layer, u, u2):
    if layer > 0:
        return u * poly(u2, ASIN[layer])
    size = jnp.abs(u)
    big = size > 0.5
    z = jnp.where(big, 0.5 - 0.5 * size, u2)
    s = jnp.where(big, z * lax.rsqrt(z), size)
    p = s * poly(z, ASIN[0])
    p = jnp.where(big, 1.0 - 2.0 * p, p)
    return jnp.where(u < 0.0, -p, p)


def norm_layers(p):
    scales, slopes = [], []
    chain = jnp.ones_like(p)
    for layer in range(LAYERS):
        spread = 1.0 + 2.0 * p
        inv = 1.0 / spread
        scales.append(lax.rsqrt(spread))
        slopes.append(chain * inv)
        if layer < LAYERS - 1:
            chain = chain * (2.0 * TWO_PI) * inv * lax.rsqrt(1.0 + 4.0 * p)
            u = 2.0 * p * inv
            p = scaled_asin(layer, u, u * u)
    return scales, slopes


def ntk_value(g, left, right):
    theta = g
    for layer in range(LAYERS):
        c2 = 2.0 * left[layer] * right[layer]
        u = g * c2
        u2 = u * u
        w = lax.rsqrt(1.0 - u2)
        g = scaled_asin(layer, u, u2)
        theta = g + theta * (TWO_PI * c2 * w)
    return theta


def ntk_full(g, left2, right, slope):
    theta = g
    dg = tg = gr = tr = None
    for layer in range(LAYERS):
        last = layer == LAYERS - 1
        c2 = left2[layer] * right[layer]
        u = g * c2
        u2 = u * u
        w = lax.rsqrt(1.0 - u2)
        cw2 = c2 * w
        step = TWO_PI * cw2
        bend = u * (w * cw2)
        ww = w * w
        tb = theta * bend
        gs = g * slope[layer]
        if layer == 0:
            tg_next = step * (2.0 + tb)
            dg_next = step
            base = -gs
            tr_next = step * (base - theta * (ww * slope[layer]))
        else:
            tg_next = step * (dg + tg + tb * dg)
            dg_next = step * dg
            base = gr - gs
            tr_next = step * (base + tr + (tb * gr - theta * (ww * slope[layer])))
        gr_next = step * base
        g = scaled_asin(layer, u, u2)
        theta = g + step * theta
        tg, dg, gr, tr = tg_next, dg_next, gr_next, tr_next
    return theta, tg, tr


def dot(a, b, dims=NN, precision=None):
    return lax.dot_general(a, b, dims, precision=precision, preferred_element_type=F32)


def split(x):
    high = x.astype(BF16)
    return high, (x - high.astype(F32)).astype(BF16)


def dot3(a, b, dims=NN):
    return dot(a[0], b[0], dims) + (dot(a[0], b[1], dims) + dot(a[1], b[0], dims))


def load_images(gathered, sup, sems):
    half = D // 2
    copies = []
    for y in range(4):
        for x in range(4):
            rows = pl.ds(32 * (y * 4 + x), 32)
            for h, slot in ((0, y * 4 + x), (1, x * 4 + y)):
                dst = sup.at[rows, h * half:(h + 1) * half]
                copies.append(pltpu.make_async_copy(gathered.at[h, slot], dst, sems.at[len(copies)]))
    for copy in copies:
        copy.start()
    return copies


def compute_kernel(
    lab_s, lab_t, gathered, tgt,
    grad, slab, inv, system, coef_t, coef_n, own_tg, own_tr,
    sup, gram, gram_ss, kern, tg_s, tr_s, coef, quant, quant_t, left_s, sq, mid, acc, sems,
):
    for copy in load_images(gathered, sup, sems):
        copy.wait()
    n_sup = sup.shape[0]
    n_tgt = tgt.shape[0]
    total_tgt = n_tgt * lax.axis_size("sup") * lax.axis_size("tgt")
    own_rows = own_tg.shape[0]

    for j in range(n_sup // 256):
        gram_ss[:, j * 256:(j + 1) * 256] = dot(sup[...], sup[j * 256:(j + 1) * 256, :], NT) * (1.0 / D)

    def gram_tile(j, carry):
        rows = pl.ds(pl.multiple_of(j * 256, 256), 256)
        gram[:, rows] = dot(sup[...], tgt[rows, :], NT) * (1.0 / D)
        return carry

    lax.fori_loop(0, n_tgt // 256, gram_tile, 0)

    def square_tile(j, carry):
        rows = pl.ds(pl.multiple_of(j * 64, 64), 64)
        total = jnp.zeros((64, 128), F32)
        for k in range(D // 128):
            x = tgt[rows, k * 128:(k + 1) * 128].astype(F32)
            total = total + x * x
        sq[rows, :] = total
        return carry

    lax.fori_loop(0, n_tgt // 64, square_tile, 0)
    norm_t = dot(jnp.full((8, 128), 1.0 / D, F32), sq[...], NT, HI)
    scales_t, unused = norm_layers(norm_t)
    for layer in range(LAYERS):
        left_s[layer] = 2.0 * scales_t[layer]
    row_id = lax.broadcasted_iota(jnp.int32, (n_sup, n_sup), 0)
    col_id = lax.broadcasted_iota(jnp.int32, (n_sup, n_sup), 1)
    diagonal = row_id == col_id
    norm_s = jnp.sum(jnp.where(diagonal, gram_ss[...], 0.0), axis=0, keepdims=True)
    scales_s, slopes_s = norm_layers(jnp.broadcast_to(norm_s, (8, n_sup)))
    quant[...] = jnp.zeros_like(quant)
    for layer in range(LAYERS):
        quant[layer * 8:layer * 8 + 8, :] = scales_s[layer]
        quant[64 + layer * 8:72 + layer * 8, :] = slopes_s[layer]
    quant_t[...] = quant[...].T

    def ss_tile(i, carry):
        rows = pl.ds(pl.multiple_of(i * 32, 32), 32)
        q = quant_t[rows, :]
        left = [q[:, l * 8:l * 8 + 1] for l in range(LAYERS)]
        right = [quant[l * 8:l * 8 + 1, :] for l in range(LAYERS)]
        system[rows, :] = ntk_value(gram_ss[rows, :], left, right)
        return carry

    lax.fori_loop(0, n_sup // 32, ss_tile, 0)
    def own_tile(i, carry):
        here = pl.ds(pl.multiple_of(i * 8, 8), 8)
        own = pl.ds(pl.multiple_of(lax.axis_index("sup") * own_rows + i * 8, 8), 8)
        q = quant_t[own, :]
        left = [q[:, l * 8:l * 8 + 1] for l in range(LAYERS)]
        slope = [q[:, 64 + l * 8:65 + l * 8] for l in range(LAYERS)]
        right2 = [2.0 * quant[l * 8:l * 8 + 8, :] for l in range(LAYERS)]
        unused, tg, tr = ntk_full(gram_ss[own, :], right2, left, slope)
        own_tg[here, :] = tg
        own_tr[here, :] = tr
        return carry

    lax.fori_loop(0, own_rows // 8, own_tile, 0)

    half = 512

    def ts_tile(t, carry):
        i, j = t // (n_tgt // half), t % (n_tgt // half)
        rows = pl.ds(pl.multiple_of(i * 8, 8), 8)
        lanes = pl.ds(pl.multiple_of(j * half, half), half)
        q = quant_t[rows, :]
        right = [q[:, l * 8:l * 8 + 1] for l in range(LAYERS)]
        slope = [q[:, 64 + l * 8:65 + l * 8] for l in range(LAYERS)]
        left2 = [left_s[l, :, lanes] for l in range(LAYERS)]
        theta, tg, tr = ntk_full(gram[rows, lanes], left2, right, slope)
        kern[rows, lanes] = theta
        tg_s[rows, lanes] = tg
        tr_s[rows, lanes] = tr
        return carry

    lax.fori_loop(0, (n_sup // 8) * (n_tgt // half), ts_tile, 0, unroll=2)

    kern_ss = system[...]
    trace = jnp.sum(jnp.sum(jnp.where(diagonal, kern_ss, 0.0), axis=0, keepdims=True), axis=1, keepdims=True)
    inv_t = n_sup / trace
    system[...] = kern_ss * inv_t + jnp.where(diagonal, RIDGE, 0.0)
    norms = jnp.sum(jnp.abs(system[...]), axis=0, keepdims=True)
    high = jnp.minimum(jnp.max(norms, axis=1, keepdims=True), n_sup + RIDGE)
    alpha = 2.0 / (high + RIDGE)
    rho = (high - RIDGE) / (high + RIDGE)
    gain = 2.0 / (2.0 - rho * rho)
    inv[...] = (gain * alpha) * (jnp.where(diagonal, 2.0, 0.0) - alpha * system[...])
    rho = 0.5 * gain * rho * rho

    def newton(k, rho):
        a = split(system[...])
        x = split(inv[...])
        mid[...] = jnp.where(diagonal, 2.0, 0.0) - dot3(a, x)
        gain = 2.0 / (2.0 - rho * rho)
        inv[...] = gain * dot3(x, split(mid[...]))
        return 0.5 * gain * rho * rho

    lax.fori_loop(0, NEWTON, newton, rho)
    inv[...] = inv[...] * inv_t
    system[...] = system[...] * (trace * (1.0 / n_sup))

    class_id = lax.broadcasted_iota(jnp.int32, (CLS, n_sup), 0)
    label = jnp.where(class_id == lab_s[...], 1.0, 0.0) - 1.0 / C
    label = jnp.where(class_id < C, label, 0.0)
    coef_t[...] = dot(label, inv[...], NN, HI)
    for k in range(REFINE):
        left_over = label - dot(coef_t[...], system[...], NN, HI)
        coef_t[...] = coef_t[...] + dot(left_over, inv[...], NN, HI)
    coef_n[...] = coef_t[...].T

    class_id = lax.broadcasted_iota(jnp.int32, (CLS, n_tgt), 0)
    label = jnp.where(class_id == lab_t[...], 1.0, 0.0) - 1.0 / C
    label = jnp.where(class_id < C, label, 0.0)
    misfit = dot(coef_t[...], kern[...], NN, HI) - label
    loss = jnp.sum(jnp.sum(misfit * misfit, axis=0, keepdims=True), axis=1, keepdims=True) * (0.5 / total_tgt)
    d_predict = misfit * (1.0 / total_tgt)
    d_coef = dot(kern[...], d_predict, NT, HI)
    gram[...] = dot(coef_n[...], d_predict, NN, HI)

    def pull_tile(i, carry):
        rows = pl.ds(pl.multiple_of(i * 16, 16), 16)
        d_kern = gram[rows, :]
        part = (d_kern * tg_s[rows, :] * (1.0 / D)).astype(BF16)
        coef[0, rows, :] = part
        block = i // 2
        other = (block % 4) * 4 + block // 4
        coef[1, pl.ds(pl.multiple_of(other * 32 + (i % 2) * 16, 16), 16), :] = part
        through = d_kern * tr_s[rows, :]
        total = through[:, :128]
        for k in range(1, n_tgt // 128):
            total = total + through[:, k * 128:(k + 1) * 128]
        acc[rows, :] = total
        return carry

    lax.fori_loop(0, n_sup // 16, pull_tile, 0)
    d_norm = jnp.sum(acc[...], axis=1, keepdims=True)
    lane = lax.broadcasted_iota(jnp.int32, (n_sup, CLS), 1)
    d_coef = jnp.where(lane == C, loss, d_coef)
    acc[...] = jnp.where(lane == C + 1, d_norm, d_coef)
    slab[0] = acc[...]
    for y in range(4):
        for x in range(4):
            slab[1, 32 * (x * 4 + y):32 * (x * 4 + y) + 32, :] = acc[32 * (y * 4 + x):32 * (y * 4 + x) + 32, :]

    for h in range(2):
        def grad_tile(j, carry):
            there = pl.ds(pl.multiple_of(j * 512, 512), 512)
            lanes = pl.ds(pl.multiple_of(j * 512 + h * (D // 2), 512), 512)
            grad[h, :, there] = dot(coef[h], tgt[:, lanes]).astype(grad.dtype)
            return carry

        lax.fori_loop(0, D // 1024, grad_tile, 0)


def compute(gathered, target_images, lab_s, lab_t, own_rows):
    n_sup, n_tgt = gathered.size // D, target_images.shape[0]
    shapes = [
        ((2, n_sup, D // 2), BF16), ((2, n_sup, CLS), F32), ((n_sup, n_sup), F32), ((n_sup, n_sup), F32),
        ((CLS, n_sup), F32), ((n_sup, CLS), F32), ((own_rows, n_sup), F32), ((own_rows, n_sup), F32),
    ]
    vmem = pl.BlockSpec(memory_space=pltpu.VMEM)
    return pl.pallas_call(
        compute_kernel,
        out_shape=[jax.ShapeDtypeStruct(s, t) for s, t in shapes],
        in_specs=[vmem, vmem, pl.BlockSpec(memory_space=pl.ANY), vmem],
        out_specs=[vmem] * len(shapes),
        scratch_shapes=[
            pltpu.VMEM((n_sup, D), BF16),
            pltpu.VMEM((n_sup, n_tgt), F32), pltpu.VMEM((n_sup, n_sup), F32),
            pltpu.VMEM((n_sup, n_tgt), F32), pltpu.VMEM((n_sup, n_tgt), F32), pltpu.VMEM((n_sup, n_tgt), F32),
            pltpu.VMEM((2, n_sup, n_tgt), BF16),
            pltpu.VMEM((128, n_sup), F32), pltpu.VMEM((n_sup, 128), F32),
            pltpu.VMEM((LAYERS, 8, n_tgt), F32), pltpu.VMEM((n_tgt, 128), F32),
            pltpu.VMEM((n_sup, n_sup), F32), pltpu.VMEM((n_sup, 128), F32),
            pltpu.SemaphoreType.DMA((32,)),
        ],
        compiler_params=pltpu.CompilerParams(vmem_limit_bytes=56 * 2**20),
        name="compute",
    )(lab_s, lab_t, gathered, target_images)


MESH = pl.DeviceIdType.MESH
RING = 4


def place():
    tgt, sup = lax.axis_index("tgt"), lax.axis_index("sup")
    core = tgt % 2
    zh = sup % RING
    x = (sup // RING) % RING
    y = sup // (RING * RING)
    a = y + core * (x - y)
    b = x + core * (y - x)
    step_a, step_b = RING - (RING - 1) * core, 1 + (RING - 1) * core

    def device(a_there, b_there, zh_there):
        return (tgt, (a_there * step_a + b_there * step_b) * RING + zh_there)

    partner = (tgt + 1 - 2 * core, sup)
    beside = ((tgt + 2) % 4, sup)
    return core, y, x, a, b, zh, device, partner, beside


def turn(index, by):
    return (index + by) % RING


def greet(devices):
    barrier = pltpu.get_barrier_semaphore()
    for device in devices:
        pl.semaphore_signal(barrier, inc=1, device_id=device, device_id_type=MESH)
    pl.semaphore_wait(barrier, len(devices))


class Sender:
    def __init__(self, send_sems, recv_sems):
        self.send_sems, self.recv_sems, self.made = send_sems, recv_sems, []

    def start(self, src, dst, device):
        k = len(self.made)
        copy = pltpu.make_async_remote_copy(
            src_ref=src, dst_ref=dst, send_sem=self.send_sems.at[k], recv_sem=self.recv_sems.at[k],
            device_id=device, device_id_type=MESH)
        copy.start()
        self.made.append(copy)
        return copy

    def drain(self):
        for copy in self.made:
            copy.wait_send()


def ring_gather(sender, block, me, left, right, then=None):
    then = then or (lambda ref: None)
    low, high = pl.ds(0, 2), pl.ds(2, 2)
    to_right = sender.start(block(me), block(me), right)
    to_left = sender.start(block(me), block(me), left)
    to_right.wait_recv()
    before = block(turn(me, 3))
    far_right = sender.start(before.at[low], before.at[low], right)
    to_left.wait_recv()
    after = block(turn(me, 1))
    far_left = sender.start(after.at[high], after.at[high], left)
    then(before)
    then(after)
    far = block(turn(me, 2))
    far_right.wait_recv()
    then(far.at[low])
    far_left.wait_recv()
    then(far.at[high])


def gather_kernel(own, out, send_sems, recv_sems, local_sem):
    core, y, x, a, b, zh, device, partner, beside = place()
    greet(
        [device(a, b, turn(zh, k)) for k in (1, 2, 3)]
        + [device(a, turn(b, k), zh) for k in (1, 3)] + [device(turn(a, k), b, zh) for k in (1, 3)] + [partner]
    )
    half = out.shape[-1]
    mine = own.at[:, pl.ds(pl.multiple_of(core * half, 128), half)]
    sender = Sender(send_sems, recv_sems)
    first = [sender.start(mine, out.at[core, a, b, zh], device(a, b, turn(zh, k))) for k in (1, 3, 2)]
    local = pltpu.make_async_copy(mine, out.at[core, a, b, zh], local_sem)
    local.start()
    local.wait()
    for copy in first:
        copy.wait_recv()
    ring_gather(sender, lambda i: out.at[core, a, i], b, device(a, turn(b, 3), zh), device(a, turn(b, 1), zh))
    across = []

    def share(ref):
        across.append(sender.start(ref, ref, partner))

    share(out.at[core, a])
    ring_gather(sender, lambda i: out.at[core, i], a, device(turn(a, 3), b, zh), device(turn(a, 1), b, zh), share)
    for copy in across:
        copy.wait_recv()
    sender.drain()


def gather_images(support_images):
    rows = support_images.shape[0]
    return pl.pallas_call(
        gather_kernel,
        out_shape=jax.ShapeDtypeStruct((2, RING, RING, RING, rows, D // 2), BF16),
        in_specs=[pl.BlockSpec(memory_space=pl.ANY)],
        out_specs=pl.BlockSpec(memory_space=pl.ANY),
        scratch_shapes=[pltpu.SemaphoreType.DMA((16,)), pltpu.SemaphoreType.DMA((16,)), pltpu.SemaphoreType.DMA],
        compiler_params=pltpu.CompilerParams(collective_id=0, has_side_effects=True),
        name="gather",
    )(support_images)


def add_blocks(dst, parts, lead):
    count = math.prod(lead)

    def one(t, carry):
        index = []
        for length in reversed(lead):
            index.append(t % length)
            t = t // length
        index = tuple(reversed(index))
        total = dst[index].astype(F32)
        for part in parts:
            total = total + part[index].astype(F32)
        dst[index] = total.astype(dst.dtype)
        return carry

    lax.fori_loop(0, count, one, 0)


class Scatter:
    def __init__(self, mine, work, near_a, far_a, near_b, far_b, tail, near_z, ends):
        self.mine, self.work, self.near_a, self.far_a = mine, work, near_a, far_a
        self.near_b, self.far_b, self.tail, self.near_z, self.ends = near_b, far_b, tail, near_z, ends


def ring_scatter_start(sender, near, block, me, left, right):
    far = block(turn(me, 2))
    to_right = sender.start(far.at[pl.ds(0, 2)], near.at[0], right)
    to_left = sender.start(far.at[pl.ds(2, 2)], near.at[1], left)
    return to_right, to_left


def ring_scatter_middle(sender, near, landing, block, me, left, right, copies, lead):
    to_right, to_left = copies
    after, before = block(turn(me, 1)), block(turn(me, 3))
    to_right.wait_recv()
    add_blocks(after.at[pl.ds(0, 2)], [near.at[0]], (2,) + lead)
    second_right = sender.start(after, landing.at[0], right)
    to_left.wait_recv()
    add_blocks(before.at[pl.ds(2, 2)], [near.at[1]], (2,) + lead)
    second_left = sender.start(before, landing.at[1], left)
    return second_right, second_left


def receive(copies):
    for copy in copies:
        copy.wait_recv()


def finish_kernel(
    grad, slab, inv_hbm, system_hbm, gathered, images, coef_t, coef_n, own_tg, own_tr,
    out, loss,
    mine, work, near_a, far_a, near_b, far_b, tail, near_z, ends, done,
    sum_own, sum_work, sum_a, sum_b, sum_z, sum_all, total, adjoint,
    inv, system, sup, part,
    send_sems, recv_sems, sum_send, sum_recv, load_sems, sup_sems,
):
    core, y, x, a, b, zh, device, partner, beside = place()
    tgt_id = lax.axis_index("tgt")
    place_z = zh * 2 + tgt_id // 2

    def along_z(k):
        there = (place_z + k) % 8
        return ((there % 2) * 2 + core, (y * RING + x) * RING + there // 2)

    rows = images.shape[0]
    n_sup = inv.shape[0]
    half = D // 2
    loads = [
        pltpu.make_async_copy(slab.at[core, :, :, pl.ds(2 * core, 2)], sum_own, load_sems.at[0]),
        pltpu.make_async_copy(grad.at[core], mine, load_sems.at[1]),
        pltpu.make_async_copy(inv_hbm, inv, load_sems.at[2]),
        pltpu.make_async_copy(system_hbm, system, load_sems.at[3]),
    ]
    for copy in loads:
        copy.start()
    images_in = load_images(gathered, sup, sup_sems)
    greet(
        [device(turn(a, k), b, zh) for k in (1, 2, 3)] + [device(a, turn(b, k), zh) for k in (1, 2, 3)]
        + [along_z(k) for k in range(1, 8)] + [partner]
    )
    sums = Sender(sum_send, sum_recv)
    sender = Sender(send_sems, recv_sems)
    left_a, right_a = device(turn(a, 3), b, zh), device(turn(a, 1), b, zh)
    left_b, right_b = device(a, turn(b, 3), zh), device(a, turn(b, 1), zh)

    pair_sum = sums.start(slab.at[1 - core, :, :, pl.ds(2 - 2 * core, 2)], sum_work, partner)
    pair = {}
    for k in (2, 1, 3, 0):
        there = turn(b, k)
        pair[k] = sender.start(grad.at[1 - core, there], work.at[there], partner)

    def add_pair(k):
        pair[k].wait_recv()
        here = turn(a, k)
        add_blocks(work.at[here], [mine.at[here]], (RING, RING))

    def at_a(i):
        return work.at[i]

    def at_b(i):
        return work.at[a, i]

    loads[0].wait()
    pair_sum.wait_recv()
    add_blocks(sum_work, [sum_own], (RING, RING, 2))
    hop = [sums.start(sum_work.at[turn(a, k)], sum_a.at[k - 1], device(turn(a, k), b, zh)) for k in (2, 1, 3)]
    loads[1].wait()
    add_pair(2)
    first = ring_scatter_start(sender, near_a, at_a, a, left_a, right_a)
    receive(hop)
    add_blocks(sum_work.at[a], [sum_a.at[0], sum_a.at[1], sum_a.at[2]], (RING, 2))
    hop = [sums.start(sum_work.at[a, turn(b, k)], sum_b.at[k - 1], device(a, turn(b, k), zh)) for k in (2, 1, 3)]
    add_pair(1)
    add_pair(3)
    receive(hop)
    sum_z[place_z] = sum_work[a, b] + sum_b[0] + sum_b[1] + sum_b[2]
    hop = [sums.start(sum_z.at[place_z], sum_z.at[place_z], along_z(k)) for k in range(1, 8)]
    second = ring_scatter_middle(sender, near_a, far_a, at_a, a, left_a, right_a, first, (RING,))
    receive(hop)
    whole = sum_z[0]
    for k in range(1, 8):
        whole = whole + sum_z[k]
    sum_all[core, a, b] = whole
    spot = sum_all.at[core, a, b]
    hop = [sums.start(spot, spot, device(a, turn(b, k), zh)) for k in (2, 1, 3)]
    add_pair(0)
    receive(hop)
    spot = sum_all.at[core, a]
    hop = [sums.start(spot, spot, device(turn(a, k), b, zh)) for k in (2, 1, 3)]
    receive(hop)
    spot = sum_all.at[core]
    pair_sum = sums.start(spot, spot, partner)
    receive(second)
    add_blocks(work.at[a], [far_a.at[0], far_a.at[1]], (RING, RING))
    first = ring_scatter_start(sender, near_b, at_b, b, left_b, right_b)
    pair_sum.wait_recv()

    for i in range(RING):
        for j in range(RING):
            base = 4 * rows * (i * RING + j)
            total[base:base + 2 * rows, :] = sum_all[0, i, j].reshape(2 * rows, CLS)
            total[base + 2 * rows:base + 4 * rows, :] = sum_all[1, j, i].reshape(2 * rows, CLS)
    loads[2].wait()
    loads[3].wait()
    lane = lax.broadcasted_iota(jnp.int32, (n_sup, CLS), 1)
    adjoint[...] = dot(inv[...], jnp.where(lane < C, total[...], 0.0), NN, HI)
    second = ring_scatter_middle(sender, near_b, far_b, at_b, b, left_b, right_b, first, ())
    left_over = jnp.where(lane < C, total[...], 0.0) - dot(system[...], adjoint[...], NN, HI)
    adjoint[...] = adjoint[...] + dot(inv[...], left_over, NN, HI)
    receive(second)
    for i in range(RING):
        tail[i] = work[a, b, i].astype(F32) + far_b[0, i].astype(F32) + far_b[1, i].astype(F32)
    third = [sender.start(tail.at[turn(zh, k)], near_z.at[k - 1], device(a, b, turn(zh, k))) for k in (2, 1, 3)]
    for k in range(REFINE - 1):
        left_over = jnp.where(lane < C, total[...], 0.0) - dot(system[...], adjoint[...], NN, HI)
        adjoint[...] = adjoint[...] + dot(inv[...], left_over, NN, HI)
    receive(third)
    ends[0] = tail[zh] + near_z[0] + (near_z[1] + near_z[2])
    fourth = sender.start(ends.at[0], ends.at[1], beside)

    start = pl.multiple_of(lax.axis_index("sup") * rows, 8)
    own = pl.ds(start, rows)
    adj = adjoint[...]
    ridge = jnp.sum(jnp.sum(adj * coef_n[...], axis=0, keepdims=True), axis=1, keepdims=True) * (-RIDGE / n_sup)
    row_id = lax.broadcasted_iota(jnp.int32, (rows, n_sup), 0) + start
    col_id = lax.broadcasted_iota(jnp.int32, (rows, n_sup), 1)
    d_kern = jnp.where(row_id == col_id, 2.0 * ridge, 0.0) - dot(adjoint[own, :], coef_t[...], NN, HI)
    d_kern = d_kern - dot(coef_n[own, :], adj, NT, HI)
    weight = d_kern * own_tg[...] * (1.0 / D)
    lane = lax.broadcasted_iota(jnp.int32, (rows, CLS), 1)
    d_norm = jnp.sum(d_kern * own_tr[...], axis=1, keepdims=True)
    d_norm = d_norm + jnp.sum(jnp.where(lane == C + 1, total[own, :], 0.0), axis=1, keepdims=True)
    loss[...] = jnp.sum(jnp.where(lane[0:1] == C, total[0:1, :], 0.0), axis=1, keepdims=True)
    high, low = split(weight)
    fourth.wait_recv()
    done[core] = ends[0] + ends[1]
    last = sender.start(done.at[core], done.at[core], partner)
    for copy in images_in:
        copy.wait()
    for k in range(D // 512):
        lanes = slice(k * 512, (k + 1) * 512)
        some = dot(high, sup[:, lanes]) + dot(low, sup[:, lanes])
        part[:, lanes] = some + (2.0 / D) * d_norm * images[:, lanes].astype(F32)
    last.wait_recv()
    for h in range(2):
        lanes = slice(h * half, (h + 1) * half)
        out[:, lanes] = n_sup * (part[:, lanes] + done[h])
    sums.drain()
    sender.drain()


def finish(grad, slab, inv, system, gathered, images, coef_t, coef_n, own_tg, own_tr):
    rows, half, n_sup = images.shape[0], D // 2, inv.shape[0]
    vmem = pl.BlockSpec(memory_space=pltpu.VMEM)
    hbm = pl.BlockSpec(memory_space=pltpu.HBM)
    return pl.pallas_call(
        finish_kernel,
        out_shape=[jax.ShapeDtypeStruct((rows, D), F32), jax.ShapeDtypeStruct((1, 1), F32)],
        in_specs=[hbm] * 5 + [vmem] * 5,
        out_specs=[vmem] * 2,
        scratch_shapes=[
            pltpu.VMEM((RING, RING, RING, rows, half), BF16),
            pltpu.VMEM((RING, RING, RING, rows, half), BF16),
            pltpu.VMEM((2, 2, RING, rows, half), BF16),
            pltpu.VMEM((2, RING, RING, rows, half), BF16),
            pltpu.VMEM((2, 2, rows, half), BF16),
            pltpu.VMEM((2, RING, rows, half), BF16),
            pltpu.VMEM((RING, rows, half), F32),
            pltpu.VMEM((3, rows, half), F32),
            pltpu.VMEM((2, rows, half), F32),
            pltpu.VMEM((2, rows, half), F32),
            pltpu.VMEM((RING, RING, 2, rows, CLS), F32),
            pltpu.VMEM((RING, RING, 2, rows, CLS), F32),
            pltpu.VMEM((3, RING, 2, rows, CLS), F32),
            pltpu.VMEM((3, 2, rows, CLS), F32),
            pltpu.VMEM((8, 2, rows, CLS), F32),
            pltpu.VMEM((2, RING, RING, 2, rows, CLS), F32),
            pltpu.VMEM((n_sup, CLS), F32),
            pltpu.VMEM((n_sup, CLS), F32),
            pltpu.VMEM((n_sup, n_sup), F32),
            pltpu.VMEM((n_sup, n_sup), F32),
            pltpu.VMEM((n_sup, D), BF16),
            pltpu.VMEM((rows, D), F32),
            pltpu.SemaphoreType.DMA((20,)), pltpu.SemaphoreType.DMA((20,)),
            pltpu.SemaphoreType.DMA((24,)), pltpu.SemaphoreType.DMA((24,)),
            pltpu.SemaphoreType.DMA((4,)), pltpu.SemaphoreType.DMA((32,)),
        ],
        compiler_params=pltpu.CompilerParams(
            collective_id=1, has_side_effects=True, vmem_limit_bytes=48 * 2**20),
        name="finish",
    )(
        grad.reshape(2, RING, RING, RING, rows, half), slab.reshape(2, RING, RING, RING, rows, CLS),
        inv, system, gathered, images, coef_t, coef_n, own_tg, own_tr)


def body(support_images, target_images, support_labels, target_labels):
    own_rows = support_images.shape[0]
    lab_s = support_labels.reshape(1, -1)
    lab_t = target_labels.reshape(1, -1)
    gathered = gather_images(support_images).reshape(2, RING * RING, RING * own_rows, D // 2)
    grad, slab, inv, system, *rest = compute(gathered, target_images, lab_s, lab_t, own_rows)
    out, loss = finish(grad, slab, inv, system, gathered, support_images, *rest)
    return out, loss[0, 0]


def solution(mesh):
    in_specs = (P("sup", None), P(("tgt", "sup"), None), P(), P(("tgt", "sup")))
    out_specs = (P("sup", None), P())
    return jax.shard_map(body, mesh=mesh, in_specs=in_specs, out_specs=out_specs, check_vma=False)
```

```python
import functools
import math

import jax
import jax.numpy as jnp
from jax import lax
from jax.experimental import pallas as pl
from jax.experimental.pallas import tpu as pltpu
from jax.sharding import PartitionSpec as P

D = 3072
C = 100
LAYERS = 5
CLS = 128
RIDGE = 0.1
TWO_PI = 2.0 / math.pi
NEWTON = 7
NEWTON_TILES = 9
REFINE = 2
HI = lax.Precision.HIGHEST
NN = (((1,), (0,)), ((), ()))
NT = (((1,), (1,)), ((), ()))
F32 = jnp.float32
BF16 = jnp.bfloat16

ASIN = (
    (1.0, 0.1666678637266159, 0.0749453455209732, 0.0455390103161335, 0.02390936389565468, 0.042553599923849106),
    (1.0, 0.16666781902313232, 0.07494797557592392, 0.04552660509943962, 0.02313542366027832, 0.0537058524787426, -0.05348314717411995, 0.08573318272829056),
    (1.0, 0.16666752099990845, 0.07495901733636856, 0.04535885155200958, 0.024863531813025475, 0.04080614075064659),
    (1.0, 0.16666492819786072, 0.0750882476568222, 0.043096426874399185, 0.04107564687728882),
    (1.0, 0.16666613519191742, 0.07503537833690643, 0.043817341327667236, 0.03804752230644226),
)


def poly(z, coefs):
    total = coefs[-1] * TWO_PI
    for value in coefs[-2::-1]:
        total = total * z + value * TWO_PI
    return total


def scaled_asin(layer, u, u2):
    if layer > 0:
        return u * poly(u2, ASIN[layer])
    size = jnp.abs(u)
    big = size > 0.5
    z = jnp.where(big, 0.5 - 0.5 * size, u2)
    s = jnp.where(big, z * lax.rsqrt(z), size)
    p = s * poly(z, ASIN[0])
    p = jnp.where(big, 1.0 - 2.0 * p, p)
    return jnp.where(u < 0.0, -p, p)


def norm_layers(p):
    scales, slopes = [], []
    chain = jnp.ones_like(p)
    for layer in range(LAYERS):
        spread = 1.0 + 2.0 * p
        inv = 1.0 / spread
        scales.append(lax.rsqrt(spread))
        slopes.append(chain * inv)
        if layer < LAYERS - 1:
            chain = chain * (2.0 * TWO_PI) * inv * lax.rsqrt(1.0 + 4.0 * p)
            u = 2.0 * p * inv
            p = scaled_asin(layer, u, u * u)
    return scales, slopes


def ntk_value(g, left, right):
    theta = g
    for layer in range(LAYERS):
        c2 = 2.0 * left[layer] * right[layer]
        u = g * c2
        u2 = u * u
        w = lax.rsqrt(1.0 - u2)
        g = scaled_asin(layer, u, u2)
        theta = g + theta * (TWO_PI * c2 * w)
    return theta


def ntk_full(g, left2, right, slope):
    theta = g
    dg = tg = gr = tr = None
    for layer in range(LAYERS):
        last = layer == LAYERS - 1
        c2 = left2[layer] * right[layer]
        u = g * c2
        u2 = u * u
        w = lax.rsqrt(1.0 - u2)
        cw2 = c2 * w
        step = TWO_PI * cw2
        bend = u * (w * cw2)
        ww = w * w
        tb = theta * bend
        gs = g * slope[layer]
        if layer == 0:
            tg_next = step * (2.0 + tb)
            dg_next = step
            base = -gs
            tr_next = step * (base - theta * (ww * slope[layer]))
        else:
            tg_next = step * (dg + tg + tb * dg)
            dg_next = step * dg
            base = gr - gs
            tr_next = step * (base + tr + (tb * gr - theta * (ww * slope[layer])))
        gr_next = step * base
        g = scaled_asin(layer, u, u2)
        theta = g + step * theta
        tg, dg, gr, tr = tg_next, dg_next, gr_next, tr_next
    return theta, tg, tr


def dot(a, b, dims=NN, precision=None):
    return lax.dot_general(a, b, dims, precision=precision, preferred_element_type=F32)


def split(x):
    high = x.astype(BF16)
    return high, (x - high.astype(F32)).astype(BF16)


def dot3(a, b, dims=NN):
    return dot(a[0], b[0], dims) + (dot(a[0], b[1], dims) + dot(a[1], b[0], dims))


def load_images(gathered, sup, sems):
    half = D // 2
    copies = []
    for y in range(4):
        for x in range(4):
            rows = pl.ds(32 * (y * 4 + x), 32)
            for h, slot in ((0, y * 4 + x), (1, x * 4 + y)):
                dst = sup.at[rows, h * half:(h + 1) * half]
                copies.append(pltpu.make_async_copy(gathered.at[h, slot], dst, sems.at[len(copies)]))
    for copy in copies:
        copy.start()
    return copies


def compute_kernel(
    lab_s, lab_t, gathered, tgt,
    grad, slab, inv, system, coef_t, coef_n, own_tg, own_tr,
    sup, gram, gram_ss, kern, tg_s, tr_s, coef, quant, quant_t, left_s, sq, mid, acc, sems,
):
    for copy in load_images(gathered, sup, sems):
        copy.wait()
    n_sup = sup.shape[0]
    n_tgt = tgt.shape[0]
    total_tgt = n_tgt * lax.axis_size("sup") * lax.axis_size("tgt")
    own_rows = own_tg.shape[0]

    for j in range(n_sup // 256):
        gram_ss[:, j * 256:(j + 1) * 256] = dot(sup[...], sup[j * 256:(j + 1) * 256, :], NT) * (1.0 / D)

    def gram_tile(j, carry):
        rows = pl.ds(pl.multiple_of(j * 256, 256), 256)
        gram[:, rows] = dot(sup[...], tgt[rows, :], NT) * (1.0 / D)
        return carry

    lax.fori_loop(0, n_tgt // 256, gram_tile, 0)

    def square_tile(j, carry):
        rows = pl.ds(pl.multiple_of(j * 64, 64), 64)
        total = jnp.zeros((64, 128), F32)
        for k in range(D // 128):
            x = tgt[rows, k * 128:(k + 1) * 128].astype(F32)
            total = total + x * x
        sq[rows, :] = total
        return carry

    lax.fori_loop(0, n_tgt // 64, square_tile, 0)
    norm_t = dot(jnp.full((8, 128), 1.0 / D, F32), sq[...], NT, HI)
    scales_t, unused = norm_layers(norm_t)
    for layer in range(LAYERS):
        left_s[layer] = 2.0 * scales_t[layer]
    row_id = lax.broadcasted_iota(jnp.int32, (n_sup, n_sup), 0)
    col_id = lax.broadcasted_iota(jnp.int32, (n_sup, n_sup), 1)
    diagonal = row_id == col_id
    norm_s = jnp.sum(jnp.where(diagonal, gram_ss[...], 0.0), axis=0, keepdims=True)
    scales_s, slopes_s = norm_layers(jnp.broadcast_to(norm_s, (8, n_sup)))
    quant[...] = jnp.zeros_like(quant)
    for layer in range(LAYERS):
        quant[layer * 8:layer * 8 + 8, :] = scales_s[layer]
        quant[64 + layer * 8:72 + layer * 8, :] = slopes_s[layer]
    quant_t[...] = quant[...].T

    def ss_tile(i, carry):
        rows = pl.ds(pl.multiple_of(i * 32, 32), 32)
        q = quant_t[rows, :]
        left = [q[:, l * 8:l * 8 + 1] for l in range(LAYERS)]
        right = [quant[l * 8:l * 8 + 1, :] for l in range(LAYERS)]
        system[rows, :] = ntk_value(gram_ss[rows, :], left, right)
        return carry

    lax.fori_loop(0, n_sup // 32, ss_tile, 0)
    def own_tile(i, carry):
        here = pl.ds(pl.multiple_of(i * 8, 8), 8)
        own = pl.ds(pl.multiple_of(lax.axis_index("sup") * own_rows + i * 8, 8), 8)
        q = quant_t[own, :]
        left = [q[:, l * 8:l * 8 + 1] for l in range(LAYERS)]
        slope = [q[:, 64 + l * 8:65 + l * 8] for l in range(LAYERS)]
        right2 = [2.0 * quant[l * 8:l * 8 + 8, :] for l in range(LAYERS)]
        unused, tg, tr = ntk_full(gram_ss[own, :], right2, left, slope)
        own_tg[here, :] = tg
        own_tr[here, :] = tr
        return carry

    lax.fori_loop(0, own_rows // 8, own_tile, 0)

    kern_ss = system[...]
    trace = jnp.sum(jnp.sum(jnp.where(diagonal, kern_ss, 0.0), axis=0, keepdims=True), axis=1, keepdims=True)
    inv_t = n_sup / trace
    system[...] = kern_ss * inv_t + jnp.where(diagonal, RIDGE, 0.0)
    norms = jnp.sum(jnp.abs(system[...]), axis=0, keepdims=True)
    high = jnp.minimum(jnp.max(norms, axis=1, keepdims=True), n_sup + RIDGE)
    alpha = 2.0 / (high + RIDGE)
    rho = (high - RIDGE) / (high + RIDGE)
    gain = 2.0 / (2.0 - rho * rho)
    inv[...] = (gain * alpha) * (jnp.where(diagonal, 2.0, 0.0) - alpha * system[...])
    rho = 0.5 * gain * rho * rho

    half = 512

    def ts_tile(i, j):
        rows = pl.ds(pl.multiple_of(i * 8, 8), 8)
        lanes = pl.ds(j * half, half)
        q = quant_t[rows, :]
        right = [q[:, l * 8:l * 8 + 1] for l in range(LAYERS)]
        slope = [q[:, 64 + l * 8:65 + l * 8] for l in range(LAYERS)]
        left2 = [left_s[l, :, lanes] for l in range(LAYERS)]
        theta, tg, tr = ntk_full(gram[rows, lanes], left2, right, slope)
        kern[rows, lanes] = theta
        tg_s[rows, lanes] = tg
        tr_s[rows, lanes] = tr


    each = NEWTON_TILES

    def newton(k, rho):
        for i in range(each):
            for j in range(n_tgt // half):
                ts_tile(k * each + i, j)
        a = split(system[...])
        x = split(inv[...])
        mid[...] = jnp.where(diagonal, 2.0, 0.0) - dot3(a, x)
        gain = 2.0 / (2.0 - rho * rho)
        inv[...] = gain * dot3(x, split(mid[...]))
        return 0.5 * gain * rho * rho

    lax.fori_loop(0, NEWTON, newton, rho)

    def ts_rest(i, carry):
        for j in range(n_tgt // half):
            ts_tile(i, j)
        return carry

    lax.fori_loop(NEWTON * each, n_sup // 8, ts_rest, 0)
    inv[...] = inv[...] * inv_t
    system[...] = system[...] * (trace * (1.0 / n_sup))

    class_id = lax.broadcasted_iota(jnp.int32, (CLS, n_sup), 0)
    label = jnp.where(class_id == lab_s[...], 1.0, 0.0) - 1.0 / C
    label = jnp.where(class_id < C, label, 0.0)
    coef_t[...] = dot(label, inv[...], NN, HI)
    for k in range(REFINE):
        left_over = label - dot(coef_t[...], system[...], NN, HI)
        coef_t[...] = coef_t[...] + dot(left_over, inv[...], NN, HI)
    coef_n[...] = coef_t[...].T

    class_id = lax.broadcasted_iota(jnp.int32, (CLS, n_tgt), 0)
    label = jnp.where(class_id == lab_t[...], 1.0, 0.0) - 1.0 / C
    label = jnp.where(class_id < C, label, 0.0)
    misfit = dot(coef_t[...], kern[...], NN, HI) - label
    loss = jnp.sum(jnp.sum(misfit * misfit, axis=0, keepdims=True), axis=1, keepdims=True) * (0.5 / total_tgt)
    d_predict = misfit * (1.0 / total_tgt)
    d_coef = dot(kern[...], d_predict, NT, HI)
    gram[...] = dot(coef_n[...], d_predict, NN, HI)

    def pull_tile(i, carry):
        rows = pl.ds(pl.multiple_of(i * 16, 16), 16)
        d_kern = gram[rows, :]
        part = (d_kern * tg_s[rows, :] * (1.0 / D)).astype(BF16)
        coef[0, rows, :] = part
        block = i // 2
        other = (block % 4) * 4 + block // 4
        coef[1, pl.ds(pl.multiple_of(other * 32 + (i % 2) * 16, 16), 16), :] = part
        through = d_kern * tr_s[rows, :]
        total = through[:, :128]
        for k in range(1, n_tgt // 128):
            total = total + through[:, k * 128:(k + 1) * 128]
        acc[rows, :] = total
        return carry

    lax.fori_loop(0, n_sup // 16, pull_tile, 0)
    d_norm = jnp.sum(acc[...], axis=1, keepdims=True)
    lane = lax.broadcasted_iota(jnp.int32, (n_sup, CLS), 1)
    d_coef = jnp.where(lane == C, loss, d_coef)
    acc[...] = jnp.where(lane == C + 1, d_norm, d_coef)
    slab[0] = acc[...]
    for y in range(4):
        for x in range(4):
            slab[1, 32 * (x * 4 + y):32 * (x * 4 + y) + 32, :] = acc[32 * (y * 4 + x):32 * (y * 4 + x) + 32, :]

    for h in range(2):
        def grad_tile(j, carry):
            there = pl.ds(pl.multiple_of(j * 512, 512), 512)
            lanes = pl.ds(pl.multiple_of(j * 512 + h * (D // 2), 512), 512)
            grad[h, :, there] = dot(coef[h], tgt[:, lanes]).astype(grad.dtype)
            return carry

        lax.fori_loop(0, D // 1024, grad_tile, 0)


def compute(gathered, target_images, lab_s, lab_t, own_rows):
    n_sup, n_tgt = gathered.size // D, target_images.shape[0]
    shapes = [
        ((2, n_sup, D // 2), BF16), ((2, n_sup, CLS), F32), ((n_sup, n_sup), F32), ((n_sup, n_sup), F32),
        ((CLS, n_sup), F32), ((n_sup, CLS), F32), ((own_rows, n_sup), F32), ((own_rows, n_sup), F32),
    ]
    vmem = pl.BlockSpec(memory_space=pltpu.VMEM)
    return pl.pallas_call(
        compute_kernel,
        out_shape=[jax.ShapeDtypeStruct(s, t) for s, t in shapes],
        in_specs=[vmem, vmem, pl.BlockSpec(memory_space=pl.ANY), vmem],
        out_specs=[vmem] * len(shapes),
        scratch_shapes=[
            pltpu.VMEM((n_sup, D), BF16),
            pltpu.VMEM((n_sup, n_tgt), F32), pltpu.VMEM((n_sup, n_sup), F32),
            pltpu.VMEM((n_sup, n_tgt), F32), pltpu.VMEM((n_sup, n_tgt), F32), pltpu.VMEM((n_sup, n_tgt), F32),
            pltpu.VMEM((2, n_sup, n_tgt), BF16),
            pltpu.VMEM((128, n_sup), F32), pltpu.VMEM((n_sup, 128), F32),
            pltpu.VMEM((LAYERS, 8, n_tgt), F32), pltpu.VMEM((n_tgt, 128), F32),
            pltpu.VMEM((n_sup, n_sup), F32), pltpu.VMEM((n_sup, 128), F32),
            pltpu.SemaphoreType.DMA((32,)),
        ],
        compiler_params=pltpu.CompilerParams(vmem_limit_bytes=36 * 2**20),
        name="compute",
    )(lab_s, lab_t, gathered, target_images)


MESH = pl.DeviceIdType.MESH
RING = 4


def place():
    tgt, sup = lax.axis_index("tgt"), lax.axis_index("sup")
    core = tgt % 2
    zh = sup % RING
    x = (sup // RING) % RING
    y = sup // (RING * RING)
    a = y + core * (x - y)
    b = x + core * (y - x)
    step_a, step_b = RING - (RING - 1) * core, 1 + (RING - 1) * core

    def device(a_there, b_there, zh_there):
        return (tgt, (a_there * step_a + b_there * step_b) * RING + zh_there)

    partner = (tgt + 1 - 2 * core, sup)
    beside = ((tgt + 2) % 4, sup)
    return core, y, x, a, b, zh, device, partner, beside


def turn(index, by):
    return (index + by) % RING


def greet(devices):
    barrier = pltpu.get_barrier_semaphore()
    for device in devices:
        pl.semaphore_signal(barrier, inc=1, device_id=device, device_id_type=MESH)
    pl.semaphore_wait(barrier, len(devices))


class Sender:
    def __init__(self, send_sems, recv_sems):
        self.send_sems, self.recv_sems, self.made = send_sems, recv_sems, []

    def start(self, src, dst, device):
        k = len(self.made)
        copy = pltpu.make_async_remote_copy(
            src_ref=src, dst_ref=dst, send_sem=self.send_sems.at[k], recv_sem=self.recv_sems.at[k],
            device_id=device, device_id_type=MESH)
        copy.start()
        self.made.append(copy)
        return copy

    def drain(self):
        for copy in self.made:
            copy.wait_send()


def gather_kernel(own, out, send_sems, recv_sems, local_sem):
    core, y, x, a, b, zh, device, partner, beside = place()
    greet(
        [device(a, b, turn(zh, k)) for k in (1, 2, 3)]
        + [device(a, turn(b, k), zh) for k in (1, 3)] + [device(turn(a, k), b, zh) for k in (1, 3)] + [partner]
    )
    half = out.shape[-1]
    mine = own.at[:, pl.ds(pl.multiple_of(core * half, 128), half)]
    sender = Sender(send_sems, recv_sems)
    first = [sender.start(mine, out.at[core, a, b, zh], device(a, b, turn(zh, k))) for k in (1, 3, 2)]
    local = pltpu.make_async_copy(mine, out.at[core, a, b, zh], local_sem)
    local.start()
    local.wait()
    for copy in first:
        copy.wait_recv()
    low, high = pl.ds(0, 2), pl.ds(2, 2)
    left_a, right_a = device(turn(a, 3), b, zh), device(turn(a, 1), b, zh)
    left_b, right_b = device(a, turn(b, 3), zh), device(a, turn(b, 1), zh)
    across = []

    def share(ref):
        across.append(sender.start(ref, ref, partner))

    def block(k, m):
        return out.at[core, turn(a, k), turn(b, m)]

    def send(ref, there):
        return sender.start(ref, ref, there)

    along_a = {}

    def launch(m):
        along_a[m] = (send(block(0, m), right_a), send(block(0, m), left_a))

    b_right, b_left = send(block(0, 0), right_b), send(block(0, 0), left_b)
    launch(0)
    share(block(0, 0))
    b_right.wait_recv()
    far_right = send(block(0, 3).at[low], right_b)
    launch(3)
    share(block(0, 3))
    b_left.wait_recv()
    far_left = send(block(0, 1).at[high], left_b)
    launch(1)
    share(block(0, 1))
    far_right.wait_recv()
    far_left.wait_recv()
    launch(2)
    share(block(0, 2))
    last = {}
    for m in (0, 3, 1, 2):
        to_right, to_left = along_a[m]
        to_right.wait_recv()
        first_half = send(block(3, m).at[low], right_a)
        share(block(3, m))
        to_left.wait_recv()
        last[m] = (first_half, send(block(1, m).at[high], left_a))
        share(block(1, m))
    for m in (0, 3, 1, 2):
        for copy in last[m]:
            copy.wait_recv()
        share(block(2, m))
    for copy in across:
        copy.wait_recv()
    sender.drain()


def gather_images(support_images):
    rows = support_images.shape[0]
    return pl.pallas_call(
        gather_kernel,
        out_shape=jax.ShapeDtypeStruct((2, RING, RING, RING, rows, D // 2), BF16),
        in_specs=[pl.BlockSpec(memory_space=pl.ANY)],
        out_specs=pl.BlockSpec(memory_space=pl.ANY),
        scratch_shapes=[pltpu.SemaphoreType.DMA((40,)), pltpu.SemaphoreType.DMA((40,)), pltpu.SemaphoreType.DMA],
        compiler_params=pltpu.CompilerParams(
            collective_id=0, has_side_effects=True, vmem_limit_bytes=4 * 2**20),
        cost_estimate=pl.CostEstimate(flops=0, bytes_accessed=80 * 2**20, transcendentals=0),
        name="gather",
    )(support_images)


def add_blocks(dst, parts, lead):
    count = math.prod(lead)

    def one(t, carry):
        index = []
        for length in reversed(lead):
            index.append(t % length)
            t = t // length
        index = tuple(reversed(index))
        if len(parts) == 1:
            dst[index] = dst[index] + parts[0][index]
            return carry
        total = dst[index].astype(F32)
        for part in parts:
            total = total + part[index].astype(F32)
        dst[index] = total.astype(dst.dtype)
        return carry

    lax.fori_loop(0, count, one, 0)


def ring_scatter_start(sender, near, block, me, left, right):
    far = block(turn(me, 2))
    to_right = sender.start(far.at[pl.ds(0, 2)], near.at[0], right)
    to_left = sender.start(far.at[pl.ds(2, 2)], near.at[1], left)
    return to_right, to_left


def ring_scatter_middle(sender, near, landing, block, me, left, right, copies, lead):
    to_right, to_left = copies
    after, before = block(turn(me, 1)), block(turn(me, 3))
    to_right.wait_recv()
    add_blocks(after.at[pl.ds(0, 2)], [near.at[0]], (2,) + lead)
    second_right = sender.start(after, landing.at[0], right)
    to_left.wait_recv()
    add_blocks(before.at[pl.ds(2, 2)], [near.at[1]], (2,) + lead)
    second_left = sender.start(before, landing.at[1], left)
    return second_right, second_left


def receive(copies):
    for copy in copies:
        copy.wait_recv()


def finish_kernel(
    grad, slab, inv, system, gathered, images, coef_t, coef_n, own_tg, own_tr,
    out, loss,
    work, near_a, far_a, near_b, far_b, tail, near_z, ends, done,
    sum_work, sum_a, sum_b, sum_z, sum_all, total, adjoint,
    sup, part,
    send_sems, recv_sems, sum_send, sum_recv, sup_sems,
):
    core, y, x, a, b, zh, device, partner, beside = place()
    tgt_id = lax.axis_index("tgt")
    place_z = zh * 2 + tgt_id // 2

    def along_z(k):
        there = (place_z + k) % 8
        return ((there % 2) * 2 + core, (y * RING + x) * RING + there // 2)

    rows = images.shape[0]
    n_sup = inv.shape[0]
    half = D // 2
    images_in = load_images(gathered, sup, sup_sems)
    greet(
        [device(turn(a, k), b, zh) for k in (1, 2, 3)] + [device(a, turn(b, k), zh) for k in (1, 2, 3)]
        + [along_z(k) for k in range(1, 8)] + [partner]
    )
    sums = Sender(sum_send, sum_recv)
    sender = Sender(send_sems, recv_sems)
    left_a, right_a = device(turn(a, 3), b, zh), device(turn(a, 1), b, zh)
    left_b, right_b = device(a, turn(b, 3), zh), device(a, turn(b, 1), zh)

    pair_sum = sums.start(slab.at[1 - core, :, :, pl.ds(2 - 2 * core, 2)], sum_work, partner)
    pair = {}
    for k in (2, 1, 3, 0):
        there = turn(b, k)
        pair[k] = sender.start(grad.at[1 - core, there], work.at[there], partner)

    def add_pair(k):
        pair[k].wait_recv()
        here = turn(a, k)
        add_blocks(work.at[here], [grad.at[core, here]], (RING, RING))

    def at_a(i):
        return work.at[i]

    def at_b(i):
        return work.at[a, i]

    pair_sum.wait_recv()
    add_blocks(sum_work, [slab.at[core, :, :, pl.ds(2 * core, 2)]], (RING, RING, 2))
    hop = [sums.start(sum_work.at[turn(a, k)], sum_a.at[k - 1], device(turn(a, k), b, zh)) for k in (2, 1, 3)]
    add_pair(2)
    first = ring_scatter_start(sender, near_a, at_a, a, left_a, right_a)
    receive(hop)
    add_blocks(sum_work.at[a], [sum_a.at[0], sum_a.at[1], sum_a.at[2]], (RING, 2))
    hop = [sums.start(sum_work.at[a, turn(b, k)], sum_b.at[k - 1], device(a, turn(b, k), zh)) for k in (2, 1, 3)]
    add_pair(1)
    add_pair(3)
    receive(hop)
    sum_z[place_z] = sum_work[a, b] + sum_b[0] + sum_b[1] + sum_b[2]
    hop = [sums.start(sum_z.at[place_z], sum_z.at[place_z], along_z(k)) for k in range(1, 8)]
    second = ring_scatter_middle(sender, near_a, far_a, at_a, a, left_a, right_a, first, (RING,))
    receive(hop)
    whole = sum_z[0]
    for k in range(1, 8):
        whole = whole + sum_z[k]
    sum_all[core, a, b] = whole
    spot = sum_all.at[core, a, b]
    hop = [sums.start(spot, spot, device(a, turn(b, k), zh)) for k in (2, 1, 3)]
    add_pair(0)
    receive(hop)
    spot = sum_all.at[core, a]
    hop = [sums.start(spot, spot, device(turn(a, k), b, zh)) for k in (2, 1, 3)]
    receive(hop)
    spot = sum_all.at[core]
    pair_sum = sums.start(spot, spot, partner)
    receive(second)
    add_blocks(work.at[a], [far_a.at[0], far_a.at[1]], (RING, RING))
    first = ring_scatter_start(sender, near_b, at_b, b, left_b, right_b)
    pair_sum.wait_recv()

    for i in range(RING):
        for j in range(RING):
            base = 4 * rows * (i * RING + j)
            total[base:base + 2 * rows, :] = sum_all[0, i, j].reshape(2 * rows, CLS)
            total[base + 2 * rows:base + 4 * rows, :] = sum_all[1, j, i].reshape(2 * rows, CLS)
    lane = lax.broadcasted_iota(jnp.int32, (n_sup, CLS), 1)
    adjoint[...] = dot(inv[...], jnp.where(lane < C, total[...], 0.0), NN, HI)
    second = ring_scatter_middle(sender, near_b, far_b, at_b, b, left_b, right_b, first, ())
    left_over = jnp.where(lane < C, total[...], 0.0) - dot(system[...], adjoint[...], NN, HI)
    adjoint[...] = adjoint[...] + dot(inv[...], left_over, NN, HI)
    receive(second)
    for i in range(RING):
        tail[i] = work[a, b, i].astype(F32) + far_b[0, i].astype(F32) + far_b[1, i].astype(F32)
    third = [sender.start(tail.at[turn(zh, k)], near_z.at[k - 1], device(a, b, turn(zh, k))) for k in (2, 1, 3)]
    for k in range(REFINE - 1):
        left_over = jnp.where(lane < C, total[...], 0.0) - dot(system[...], adjoint[...], NN, HI)
        adjoint[...] = adjoint[...] + dot(inv[...], left_over, NN, HI)
    receive(third)
    ends[0] = tail[zh] + near_z[0] + (near_z[1] + near_z[2])
    fourth = sender.start(ends.at[0], ends.at[1], beside)

    start = pl.multiple_of(lax.axis_index("sup") * rows, 8)
    own = pl.ds(start, rows)
    adj = adjoint[...]
    ridge = jnp.sum(jnp.sum(adj * coef_n[...], axis=0, keepdims=True), axis=1, keepdims=True) * (-RIDGE / n_sup)
    row_id = lax.broadcasted_iota(jnp.int32, (rows, n_sup), 0) + start
    col_id = lax.broadcasted_iota(jnp.int32, (rows, n_sup), 1)
    d_kern = jnp.where(row_id == col_id, 2.0 * ridge, 0.0) - dot(adjoint[own, :], coef_t[...], NN, HI)
    d_kern = d_kern - dot(coef_n[own, :], adj, NT, HI)
    weight = d_kern * own_tg[...] * (1.0 / D)
    lane = lax.broadcasted_iota(jnp.int32, (rows, CLS), 1)
    d_norm = jnp.sum(d_kern * own_tr[...], axis=1, keepdims=True)
    d_norm = d_norm + jnp.sum(jnp.where(lane == C + 1, total[own, :], 0.0), axis=1, keepdims=True)
    loss[...] = jnp.sum(jnp.where(lane[0:1] == C, total[0:1, :], 0.0), axis=1, keepdims=True)
    high, low = split(weight)
    fourth.wait_recv()
    done[core] = ends[0] + ends[1]
    last = sender.start(done.at[core], done.at[core], partner)
    for copy in images_in:
        copy.wait()
    for k in range(D // 512):
        lanes = slice(k * 512, (k + 1) * 512)
        some = dot(high, sup[:, lanes]) + dot(low, sup[:, lanes])
        part[:, lanes] = some + (2.0 / D) * d_norm * images[:, lanes].astype(F32)
    last.wait_recv()
    for h in range(2):
        lanes = slice(h * half, (h + 1) * half)
        out[:, lanes] = n_sup * (part[:, lanes] + done[h])
    sums.drain()
    sender.drain()


def finish(grad, slab, inv, system, gathered, images, coef_t, coef_n, own_tg, own_tr):
    rows, half, n_sup = images.shape[0], D // 2, inv.shape[0]
    vmem = pl.BlockSpec(memory_space=pltpu.VMEM)
    return pl.pallas_call(
        finish_kernel,
        out_shape=[jax.ShapeDtypeStruct((rows, D), F32), jax.ShapeDtypeStruct((1, 1), F32)],
        in_specs=[vmem] * 4 + [pl.BlockSpec(memory_space=pl.ANY)] + [vmem] * 5,
        out_specs=[vmem] * 2,
        scratch_shapes=[
            pltpu.VMEM((RING, RING, RING, rows, half), BF16),
            pltpu.VMEM((2, 2, RING, rows, half), BF16),
            pltpu.VMEM((2, RING, RING, rows, half), BF16),
            pltpu.VMEM((2, 2, rows, half), BF16),
            pltpu.VMEM((2, RING, rows, half), BF16),
            pltpu.VMEM((RING, rows, half), F32),
            pltpu.VMEM((3, rows, half), F32),
            pltpu.VMEM((2, rows, half), F32),
            pltpu.VMEM((2, rows, half), F32),
            pltpu.VMEM((RING, RING, 2, rows, CLS), F32),
            pltpu.VMEM((3, RING, 2, rows, CLS), F32),
            pltpu.VMEM((3, 2, rows, CLS), F32),
            pltpu.VMEM((8, 2, rows, CLS), F32),
            pltpu.VMEM((2, RING, RING, 2, rows, CLS), F32),
            pltpu.VMEM((n_sup, CLS), F32),
            pltpu.VMEM((n_sup, CLS), F32),
            pltpu.VMEM((n_sup, D), BF16),
            pltpu.VMEM((rows, D), F32),
            pltpu.SemaphoreType.DMA((20,)), pltpu.SemaphoreType.DMA((20,)),
            pltpu.SemaphoreType.DMA((24,)), pltpu.SemaphoreType.DMA((24,)),
            pltpu.SemaphoreType.DMA((32,)),
        ],
        compiler_params=pltpu.CompilerParams(
            collective_id=1, has_side_effects=True, vmem_limit_bytes=24 * 2**20),
        name="finish",
    )(
        grad.reshape(2, RING, RING, RING, rows, half), slab.reshape(2, RING, RING, RING, rows, CLS),
        inv, system, gathered, images, coef_t, coef_n, own_tg, own_tr)


def body(support_images, target_images, support_labels, target_labels):
    own_rows = support_images.shape[0]
    lab_s = support_labels.reshape(1, -1)
    lab_t = target_labels.reshape(1, -1)
    gathered = gather_images(support_images).reshape(2, RING * RING, RING * own_rows, D // 2)
    grad, slab, inv, system, *rest = compute(gathered, target_images, lab_s, lab_t, own_rows)
    out, loss = finish(grad, slab, inv, system, gathered, support_images, *rest)
    return out, loss[0, 0]


def solution(mesh):
    in_specs = (P("sup", None), P(("tgt", "sup"), None), P(), P(("tgt", "sup")))
    out_specs = (P("sup", None), P())
    return jax.shard_map(body, mesh=mesh, in_specs=in_specs, out_specs=out_specs, check_vma=False)
```

```python
import functools
import math

import jax
import jax.numpy as jnp
from jax import lax
from jax.experimental import pallas as pl
from jax.experimental.pallas import tpu as pltpu
from jax.sharding import PartitionSpec as P

D = 3072
C = 100
LAYERS = 5
CLS = 128
RIDGE = 0.1
TWO_PI = 2.0 / math.pi
NEWTON = 7
NEWTON_TILES = 9
REFINE = 2
HI = lax.Precision.HIGHEST
NN = (((1,), (0,)), ((), ()))
NT = (((1,), (1,)), ((), ()))
F32 = jnp.float32
BF16 = jnp.bfloat16

ASIN = (
    (1.0, 0.1666678637266159, 0.0749453455209732, 0.0455390103161335, 0.02390936389565468, 0.042553599923849106),
    (1.0, 0.1666594296693802, 0.07524710148572922, 0.04152849689126015, 0.04858245328068733, -0.02943584695458412, 0.08121654391288757),
    (1.0, 0.16665531694889069, 0.07537393271923065, 0.04041983559727669, 0.0488600954413414),
    (1.0, 0.16666492819786072, 0.0750882476568222, 0.043096426874399185, 0.04107564687728882),
    (0.9999999403953552, 0.16668136417865753, 0.07438473403453827, 0.052717722952365875),
)


def poly(z, coefs):
    total = coefs[-1] * TWO_PI
    for value in coefs[-2::-1]:
        total = total * z + value * TWO_PI
    return total


def scaled_asin(layer, u, u2):
    if layer > 0:
        return u * poly(u2, ASIN[layer])
    size = jnp.abs(u)
    big = size > 0.5
    z = jnp.where(big, 0.5 - 0.5 * size, u2)
    s = jnp.where(big, z * lax.rsqrt(z), size)
    p = s * poly(z, ASIN[0])
    p = jnp.where(big, 1.0 - 2.0 * p, p)
    return jnp.where(u < 0.0, -p, p)


def norm_layers(p):
    scales, slopes = [], []
    chain = jnp.ones_like(p)
    for layer in range(LAYERS):
        spread = 1.0 + 2.0 * p
        inv = 1.0 / spread
        scales.append(lax.rsqrt(spread))
        slopes.append(chain * inv)
        if layer < LAYERS - 1:
            chain = chain * (2.0 * TWO_PI) * inv * lax.rsqrt(1.0 + 4.0 * p)
            u = 2.0 * p * inv
            p = scaled_asin(layer, u, u * u)
    return scales, slopes


def ntk_value(g, left, right):
    theta = g
    for layer in range(LAYERS):
        c2 = 2.0 * left[layer] * right[layer]
        u = g * c2
        u2 = u * u
        w = lax.rsqrt(1.0 - u2)
        g = scaled_asin(layer, u, u2)
        theta = g + theta * (TWO_PI * c2 * w)
    return theta


def ntk_full(g, left2, right, slope):
    theta = g
    dg = tg = gr = tr = None
    for layer in range(LAYERS):
        last = layer == LAYERS - 1
        c2 = left2[layer] * right[layer]
        u = g * c2
        u2 = u * u
        w = lax.rsqrt(1.0 - u2)
        cw2 = c2 * w
        step = TWO_PI * cw2
        tw = theta * (w * w)
        tb = tw * (u * c2)
        gs = g * slope[layer]
        if layer == 0:
            tg_next = step * (2.0 + tb)
            dg_next = step
            base = -gs
            tr_next = step * (base - tw * slope[layer])
        else:
            tg_next = step * (dg + tg + tb * dg)
            dg_next = step * dg
            base = gr - gs
            tr_next = step * (base + tr + (tb * gr - tw * slope[layer]))
        gr_next = step * base
        g = scaled_asin(layer, u, u2)
        theta = g + step * theta
        tg, dg, gr, tr = tg_next, dg_next, gr_next, tr_next
    return theta, tg, tr


def dot(a, b, dims=NN, precision=None):
    return lax.dot_general(a, b, dims, precision=precision, preferred_element_type=F32)


def split(x):
    high = x.astype(BF16)
    return high, (x - high.astype(F32)).astype(BF16)


def dot3(a, b, dims=NN):
    return dot(a[0], b[0], dims) + (dot(a[0], b[1], dims) + dot(a[1], b[0], dims))


def load_images(gathered, sup, sems):
    half = D // 2
    copies = []
    for y in range(4):
        for x in range(4):
            rows = pl.ds(32 * (y * 4 + x), 32)
            for h, slot in ((0, y * 4 + x), (1, x * 4 + y)):
                dst = sup.at[rows, h * half:(h + 1) * half]
                copies.append(pltpu.make_async_copy(gathered.at[h, slot], dst, sems.at[len(copies)]))
    for copy in copies:
        copy.start()
    return copies


def compute_kernel(
    lab_s, lab_t, gathered, tgt,
    grad, slab, inv, system, coef_t, coef_n, own_tg, own_tr,
    sup, gram, gram_ss, kern, tg_s, tr_s, coef, quant, quant_t, left_s, sq, mid, acc, sems,
):
    for copy in load_images(gathered, sup, sems):
        copy.wait()
    n_sup = sup.shape[0]
    n_tgt = tgt.shape[0]
    total_tgt = n_tgt * lax.axis_size("sup") * lax.axis_size("tgt")
    own_rows = own_tg.shape[0]

    for j in range(n_sup // 256):
        gram_ss[:, j * 256:(j + 1) * 256] = dot(sup[...], sup[j * 256:(j + 1) * 256, :], NT) * (1.0 / D)

    def gram_tile(j, carry):
        rows = pl.ds(pl.multiple_of(j * 256, 256), 256)
        gram[:, rows] = dot(sup[...], tgt[rows, :], NT) * (1.0 / D)
        return carry

    lax.fori_loop(0, n_tgt // 256, gram_tile, 0)

    def square_tile(j, carry):
        rows = pl.ds(pl.multiple_of(j * 64, 64), 64)
        total = jnp.zeros((64, 128), F32)
        for k in range(D // 128):
            x = tgt[rows, k * 128:(k + 1) * 128].astype(F32)
            total = total + x * x
        sq[rows, :] = total
        return carry

    lax.fori_loop(0, n_tgt // 64, square_tile, 0)
    norm_t = dot(jnp.full((8, 128), 1.0 / D, F32), sq[...], NT, HI)
    scales_t, unused = norm_layers(norm_t)
    for layer in range(LAYERS):
        left_s[layer] = 2.0 * scales_t[layer]
    row_id = lax.broadcasted_iota(jnp.int32, (n_sup, n_sup), 0)
    col_id = lax.broadcasted_iota(jnp.int32, (n_sup, n_sup), 1)
    diagonal = row_id == col_id
    norm_s = jnp.sum(jnp.where(diagonal, gram_ss[...], 0.0), axis=0, keepdims=True)
    scales_s, slopes_s = norm_layers(jnp.broadcast_to(norm_s, (8, n_sup)))
    quant[...] = jnp.zeros_like(quant)
    for layer in range(LAYERS):
        quant[layer * 8:layer * 8 + 8, :] = scales_s[layer]
        quant[64 + layer * 8:72 + layer * 8, :] = slopes_s[layer]
    quant_t[...] = quant[...].T

    def ss_tile(i, carry):
        rows = pl.ds(pl.multiple_of(i * 32, 32), 32)
        q = quant_t[rows, :]
        left = [q[:, l * 8:l * 8 + 1] for l in range(LAYERS)]
        right = [quant[l * 8:l * 8 + 1, :] for l in range(LAYERS)]
        system[rows, :] = ntk_value(gram_ss[rows, :], left, right)
        return carry

    lax.fori_loop(0, n_sup // 32, ss_tile, 0)
    def own_tile(i, carry):
        here = pl.ds(pl.multiple_of(i * 8, 8), 8)
        own = pl.ds(pl.multiple_of(lax.axis_index("sup") * own_rows + i * 8, 8), 8)
        q = quant_t[own, :]
        left = [q[:, l * 8:l * 8 + 1] for l in range(LAYERS)]
        slope = [q[:, 64 + l * 8:65 + l * 8] for l in range(LAYERS)]
        right2 = [2.0 * quant[l * 8:l * 8 + 8, :] for l in range(LAYERS)]
        unused, tg, tr = ntk_full(gram_ss[own, :], right2, left, slope)
        own_tg[here, :] = tg
        own_tr[here, :] = tr
        return carry

    lax.fori_loop(0, own_rows // 8, own_tile, 0)

    kern_ss = system[...]
    trace = jnp.sum(jnp.sum(jnp.where(diagonal, kern_ss, 0.0), axis=0, keepdims=True), axis=1, keepdims=True)
    inv_t = n_sup / trace
    system[...] = kern_ss * inv_t + jnp.where(diagonal, RIDGE, 0.0)
    norms = jnp.sum(jnp.abs(system[...]), axis=0, keepdims=True)
    high = jnp.minimum(jnp.max(norms, axis=1, keepdims=True), n_sup + RIDGE)
    alpha = 2.0 / (high + RIDGE)
    rho = (high - RIDGE) / (high + RIDGE)
    gain = 2.0 / (2.0 - rho * rho)
    inv[...] = (gain * alpha) * (jnp.where(diagonal, 2.0, 0.0) - alpha * system[...])
    rho = 0.5 * gain * rho * rho

    half = 512

    def ts_tile(i, j):
        rows = pl.ds(pl.multiple_of(i * 8, 8), 8)
        lanes = pl.ds(j * half, half)
        q = quant_t[rows, :]
        right = [q[:, l * 8:l * 8 + 1] for l in range(LAYERS)]
        slope = [q[:, 64 + l * 8:65 + l * 8] for l in range(LAYERS)]
        left2 = [left_s[l, :, lanes] for l in range(LAYERS)]
        theta, tg, tr = ntk_full(gram[rows, lanes], left2, right, slope)
        kern[rows, lanes] = theta
        tg_s[rows, lanes] = tg
        tr_s[rows, lanes] = tr


    each = NEWTON_TILES

    def newton(k, rho):
        for i in range(each):
            for j in range(n_tgt // half):
                ts_tile(k * each + i, j)
        a = split(system[...])
        x = split(inv[...])
        mid[...] = jnp.where(diagonal, 2.0, 0.0) - dot3(a, x)
        gain = 2.0 / (2.0 - rho * rho)
        inv[...] = gain * dot3(x, split(mid[...]))
        return 0.5 * gain * rho * rho

    lax.fori_loop(0, NEWTON, newton, rho)

    def ts_rest(i, carry):
        for j in range(n_tgt // half):
            ts_tile(i, j)
        return carry

    lax.fori_loop(NEWTON * each, n_sup // 8, ts_rest, 0)
    inv[...] = inv[...] * inv_t
    system[...] = system[...] * (trace * (1.0 / n_sup))

    class_id = lax.broadcasted_iota(jnp.int32, (CLS, n_sup), 0)
    label = jnp.where(class_id == lab_s[...], 1.0, 0.0) - 1.0 / C
    label = jnp.where(class_id < C, label, 0.0)
    coef_t[...] = dot(label, inv[...], NN, HI)
    for k in range(REFINE):
        left_over = label - dot(coef_t[...], system[...], NN, HI)
        coef_t[...] = coef_t[...] + dot(left_over, inv[...], NN, HI)
    coef_n[...] = coef_t[...].T

    class_id = lax.broadcasted_iota(jnp.int32, (CLS, n_tgt), 0)
    label = jnp.where(class_id == lab_t[...], 1.0, 0.0) - 1.0 / C
    label = jnp.where(class_id < C, label, 0.0)
    misfit = dot(coef_t[...], kern[...], NN, HI) - label
    loss = jnp.sum(jnp.sum(misfit * misfit, axis=0, keepdims=True), axis=1, keepdims=True) * (0.5 / total_tgt)
    d_predict = misfit * (1.0 / total_tgt)
    d_coef = dot(kern[...], d_predict, NT, HI)
    gram[...] = dot(coef_n[...], d_predict, NN, HI)

    def pull_tile(i, carry):
        rows = pl.ds(pl.multiple_of(i * 16, 16), 16)
        d_kern = gram[rows, :]
        part = (d_kern * tg_s[rows, :] * (1.0 / D)).astype(BF16)
        coef[0, rows, :] = part
        block = i // 2
        other = (block % 4) * 4 + block // 4
        coef[1, pl.ds(pl.multiple_of(other * 32 + (i % 2) * 16, 16), 16), :] = part
        through = d_kern * tr_s[rows, :]
        total = through[:, :128]
        for k in range(1, n_tgt // 128):
            total = total + through[:, k * 128:(k + 1) * 128]
        acc[rows, :] = total
        return carry

    lax.fori_loop(0, n_sup // 16, pull_tile, 0)
    d_norm = jnp.sum(acc[...], axis=1, keepdims=True)
    lane = lax.broadcasted_iota(jnp.int32, (n_sup, CLS), 1)
    d_coef = jnp.where(lane == C, loss, d_coef)
    acc[...] = jnp.where(lane == C + 1, d_norm, d_coef)
    slab[0] = acc[...]
    for y in range(4):
        for x in range(4):
            slab[1, 32 * (x * 4 + y):32 * (x * 4 + y) + 32, :] = acc[32 * (y * 4 + x):32 * (y * 4 + x) + 32, :]

    for h in range(2):
        def grad_tile(j, carry):
            there = pl.ds(pl.multiple_of(j * 512, 512), 512)
            lanes = pl.ds(pl.multiple_of(j * 512 + h * (D // 2), 512), 512)
            grad[h, :, there] = dot(coef[h], tgt[:, lanes]).astype(grad.dtype)
            return carry

        lax.fori_loop(0, D // 1024, grad_tile, 0)


def compute(gathered, target_images, lab_s, lab_t, own_rows):
    n_sup, n_tgt = gathered.size // D, target_images.shape[0]
    shapes = [
        ((2, n_sup, D // 2), BF16), ((2, n_sup, CLS), F32), ((n_sup, n_sup), F32), ((n_sup, n_sup), F32),
        ((CLS, n_sup), F32), ((n_sup, CLS), F32), ((own_rows, n_sup), F32), ((own_rows, n_sup), F32),
    ]
    vmem = pl.BlockSpec(memory_space=pltpu.VMEM)
    return pl.pallas_call(
        compute_kernel,
        out_shape=[jax.ShapeDtypeStruct(s, t) for s, t in shapes],
        in_specs=[vmem, vmem, pl.BlockSpec(memory_space=pl.ANY), vmem],
        out_specs=[vmem] * len(shapes),
        scratch_shapes=[
            pltpu.VMEM((n_sup, D), BF16),
            pltpu.VMEM((n_sup, n_tgt), F32), pltpu.VMEM((n_sup, n_sup), F32),
            pltpu.VMEM((n_sup, n_tgt), F32), pltpu.VMEM((n_sup, n_tgt), F32), pltpu.VMEM((n_sup, n_tgt), F32),
            pltpu.VMEM((2, n_sup, n_tgt), BF16),
            pltpu.VMEM((128, n_sup), F32), pltpu.VMEM((n_sup, 128), F32),
            pltpu.VMEM((LAYERS, 8, n_tgt), F32), pltpu.VMEM((n_tgt, 128), F32),
            pltpu.VMEM((n_sup, n_sup), F32), pltpu.VMEM((n_sup, 128), F32),
            pltpu.SemaphoreType.DMA((32,)),
        ],
        compiler_params=pltpu.CompilerParams(vmem_limit_bytes=36 * 2**20),
        name="compute",
    )(lab_s, lab_t, gathered, target_images)


MESH = pl.DeviceIdType.MESH
RING = 4


def place():
    tgt, sup = lax.axis_index("tgt"), lax.axis_index("sup")
    core = tgt % 2
    zh = sup % RING
    x = (sup // RING) % RING
    y = sup // (RING * RING)
    a = y + core * (x - y)
    b = x + core * (y - x)
    step_a, step_b = RING - (RING - 1) * core, 1 + (RING - 1) * core

    def device(a_there, b_there, zh_there):
        return (tgt, (a_there * step_a + b_there * step_b) * RING + zh_there)

    partner = (tgt + 1 - 2 * core, sup)
    beside = ((tgt + 2) % 4, sup)
    return core, y, x, a, b, zh, device, partner, beside


def turn(index, by):
    return (index + by) % RING


def greet(devices):
    barrier = pltpu.get_barrier_semaphore()
    for device in devices:
        pl.semaphore_signal(barrier, inc=1, device_id=device, device_id_type=MESH)
    pl.semaphore_wait(barrier, len(devices))


class Sender:
    def __init__(self, send_sems, recv_sems):
        self.send_sems, self.recv_sems, self.made = send_sems, recv_sems, []

    def start(self, src, dst, device):
        k = len(self.made)
        copy = pltpu.make_async_remote_copy(
            src_ref=src, dst_ref=dst, send_sem=self.send_sems.at[k], recv_sem=self.recv_sems.at[k],
            device_id=device, device_id_type=MESH)
        copy.start()
        self.made.append(copy)
        return copy

    def drain(self):
        for copy in self.made:
            copy.wait_send()


def gather_kernel(own, tgt, out, tgt_near, send_sems, recv_sems, local_sem, tgt_sem):
    near = pltpu.make_async_copy(tgt, tgt_near, tgt_sem)
    near.start()
    core, y, x, a, b, zh, device, partner, beside = place()
    greet(
        [device(a, b, turn(zh, k)) for k in (1, 2, 3)]
        + [device(a, turn(b, k), zh) for k in (1, 3)] + [device(turn(a, k), b, zh) for k in (1, 3)] + [partner]
    )
    half = out.shape[-1]
    mine = own.at[:, pl.ds(pl.multiple_of(core * half, 128), half)]
    sender = Sender(send_sems, recv_sems)
    first = [sender.start(mine, out.at[core, a, b, zh], device(a, b, turn(zh, k))) for k in (1, 3, 2)]
    local = pltpu.make_async_copy(mine, out.at[core, a, b, zh], local_sem)
    local.start()
    local.wait()
    for copy in first:
        copy.wait_recv()
    low, high = pl.ds(0, 2), pl.ds(2, 2)
    left_a, right_a = device(turn(a, 3), b, zh), device(turn(a, 1), b, zh)
    left_b, right_b = device(a, turn(b, 3), zh), device(a, turn(b, 1), zh)
    across = []

    def share(ref):
        across.append(sender.start(ref, ref, partner))

    def block(k, m):
        return out.at[core, turn(a, k), turn(b, m)]

    def send(ref, there):
        return sender.start(ref, ref, there)

    along_a = {}

    def launch(m):
        along_a[m] = (send(block(0, m), right_a), send(block(0, m), left_a))

    b_right, b_left = send(block(0, 0), right_b), send(block(0, 0), left_b)
    launch(0)
    share(block(0, 0))
    b_right.wait_recv()
    far_right = send(block(0, 3).at[low], right_b)
    launch(3)
    share(block(0, 3))
    b_left.wait_recv()
    far_left = send(block(0, 1).at[high], left_b)
    launch(1)
    share(block(0, 1))
    far_right.wait_recv()
    far_left.wait_recv()
    launch(2)
    share(block(0, 2))
    last = {}
    for m in (0, 3, 1, 2):
        to_right, to_left = along_a[m]
        to_right.wait_recv()
        first_half = send(block(3, m).at[low], right_a)
        share(block(3, m))
        to_left.wait_recv()
        last[m] = (first_half, send(block(1, m).at[high], left_a))
        share(block(1, m))
    for m in (0, 3, 1, 2):
        for copy in last[m]:
            copy.wait_recv()
        share(block(2, m))
    for copy in across:
        copy.wait_recv()
    sender.drain()
    near.wait()


def gather_images(support_images, target_images):
    rows = support_images.shape[0]
    return pl.pallas_call(
        gather_kernel,
        out_shape=[
            jax.ShapeDtypeStruct((2, RING, RING, RING, rows, D // 2), BF16),
            jax.ShapeDtypeStruct(target_images.shape, BF16),
        ],
        in_specs=[pl.BlockSpec(memory_space=pl.ANY)] * 2,
        out_specs=[pl.BlockSpec(memory_space=pl.ANY)] * 2,
        scratch_shapes=[pltpu.SemaphoreType.DMA((40,)), pltpu.SemaphoreType.DMA((40,)), pltpu.SemaphoreType.DMA,
            pltpu.SemaphoreType.DMA],
        compiler_params=pltpu.CompilerParams(
            collective_id=0, has_side_effects=True, vmem_limit_bytes=41 * 2**20),
        cost_estimate=pl.CostEstimate(flops=0, bytes_accessed=80 * 2**20, transcendentals=0),
        name="gather",
    )(support_images, target_images)


def add_blocks(dst, parts, lead):
    count = math.prod(lead)

    def one(t, carry):
        index = []
        for length in reversed(lead):
            index.append(t % length)
            t = t // length
        index = tuple(reversed(index))
        if len(parts) == 1:
            dst[index] = dst[index] + parts[0][index]
            return carry
        total = dst[index].astype(F32)
        for part in parts:
            total = total + part[index].astype(F32)
        dst[index] = total.astype(dst.dtype)
        return carry

    lax.fori_loop(0, count, one, 0)


def ring_scatter_start(sender, near, block, me, left, right):
    far = block(turn(me, 2))
    to_right = sender.start(far.at[pl.ds(0, 2)], near.at[0], right)
    to_left = sender.start(far.at[pl.ds(2, 2)], near.at[1], left)
    return to_right, to_left


def ring_scatter_middle(sender, near, landing, block, me, left, right, copies, lead):
    to_right, to_left = copies
    after, before = block(turn(me, 1)), block(turn(me, 3))
    to_right.wait_recv()
    add_blocks(after.at[pl.ds(0, 2)], [near.at[0]], lead)
    second_right = sender.start(after, landing.at[0], right)
    to_left.wait_recv()
    add_blocks(before.at[pl.ds(2, 2)], [near.at[1]], lead)
    second_left = sender.start(before, landing.at[1], left)
    return second_right, second_left


def receive(copies):
    for copy in copies:
        copy.wait_recv()


def finish_kernel(
    grad, slab, inv, system, gathered, images, coef_t, coef_n, own_tg, own_tr,
    out, loss,
    work, near_a, far_a, near_b, far_b, tail, near_z, ends, done,
    sum_work, sum_a, sum_b, sum_z, sum_all, total, adjoint,
    sup, part, pieces,
    send_sems, recv_sems, sum_send, sum_recv, sup_sems,
):
    core, y, x, a, b, zh, device, partner, beside = place()
    tgt_id = lax.axis_index("tgt")
    place_z = zh * 2 + tgt_id // 2

    def along_z(k):
        there = (place_z + k) % 8
        return ((there % 2) * 2 + core, (y * RING + x) * RING + there // 2)

    rows = images.shape[0]
    n_sup = inv.shape[0]
    half = D // 2
    images_in = load_images(gathered, sup, sup_sems)
    greet(
        [device(turn(a, k), b, zh) for k in (1, 2, 3)] + [device(a, turn(b, k), zh) for k in (1, 2, 3)]
        + [along_z(k) for k in range(1, 8)] + [partner]
    )
    sums = Sender(sum_send, sum_recv)
    sender = Sender(send_sems, recv_sems)
    left_a, right_a = device(turn(a, 3), b, zh), device(turn(a, 1), b, zh)
    left_b, right_b = device(a, turn(b, 3), zh), device(a, turn(b, 1), zh)

    pair_sum = sums.start(slab.at[1 - core, :, :, pl.ds(2 - 2 * core, 2)], sum_work, partner)
    pair = {}
    for k in (2, 1, 3, 0):
        there = turn(b, k)
        pair[k] = sender.start(grad.at[1 - core, there], work.at[there], partner)

    def add_pair(k):
        pair[k].wait_recv()
        here = turn(a, k)
        add_blocks(work.at[here], [grad.at[core, here]], (RING,))

    def at_a(i):
        return work.at[i]

    def at_b(i):
        return work.at[a, i]

    pair_sum.wait_recv()
    sum_work[...] = sum_work[...] + slab[core, :, :, pl.ds(2 * core, 2)]
    hop = [sums.start(sum_work.at[turn(a, k)], sum_a.at[k - 1], device(turn(a, k), b, zh)) for k in (2, 1, 3)]
    add_pair(2)
    first = ring_scatter_start(sender, near_a, at_a, a, left_a, right_a)
    receive(hop)
    sum_work[a] = sum_work[a] + sum_a[0] + sum_a[1] + sum_a[2]
    hop = [sums.start(sum_work.at[a, turn(b, k)], sum_b.at[k - 1], device(a, turn(b, k), zh)) for k in (2, 1, 3)]
    add_pair(1)
    add_pair(3)
    receive(hop)
    sum_z[place_z] = sum_work[a, b] + sum_b[0] + sum_b[1] + sum_b[2]
    hop = [sums.start(sum_z.at[place_z], sum_z.at[place_z], along_z(k)) for k in range(1, 8)]
    second = ring_scatter_middle(sender, near_a, far_a, at_a, a, left_a, right_a, first, (2,))
    receive(hop)
    whole = sum_z[0]
    for k in range(1, 8):
        whole = whole + sum_z[k]
    sum_all[core, a, b] = whole
    spot = sum_all.at[core, a, b]
    hop = [sums.start(spot, spot, device(a, turn(b, k), zh)) for k in (2, 1, 3)]
    add_pair(0)
    receive(hop)
    spot = sum_all.at[core, a]
    hop = [sums.start(spot, spot, device(turn(a, k), b, zh)) for k in (2, 1, 3)]
    receive(hop)
    spot = sum_all.at[core]
    pair_sum = sums.start(spot, spot, partner)
    receive(second)

    def add_a(k):
        here = turn(b, k)
        add_blocks(work.at[a, here], [far_a.at[0, here], far_a.at[1, here]], (RING,))

    add_a(2)
    first = ring_scatter_start(sender, near_b, at_b, b, left_b, right_b)
    add_a(1)
    add_a(3)
    add_a(0)
    pair_sum.wait_recv()

    for i in range(RING):
        for j in range(RING):
            base = 4 * rows * (i * RING + j)
            total[base:base + 2 * rows, :] = sum_all[0, i, j].reshape(2 * rows, CLS)
            total[base + 2 * rows:base + 4 * rows, :] = sum_all[1, j, i].reshape(2 * rows, CLS)
    lane = lax.broadcasted_iota(jnp.int32, (n_sup, CLS), 1)
    adjoint[...] = dot(inv[...], jnp.where(lane < C, total[...], 0.0), NN, HI)
    second = ring_scatter_middle(sender, near_b, far_b, at_b, b, left_b, right_b, first, ())
    left_over = jnp.where(lane < C, total[...], 0.0) - dot(system[...], adjoint[...], NN, HI)
    adjoint[...] = adjoint[...] + dot(inv[...], left_over, NN, HI)
    receive(second)
    for i in range(RING):
        tail[i] = work[a, b, i].astype(F32) + far_b[0, i].astype(F32) + far_b[1, i].astype(F32)
    third = [sender.start(tail.at[turn(zh, k)], near_z.at[k - 1], device(a, b, turn(zh, k))) for k in (2, 1, 3)]
    for k in range(REFINE - 1):
        left_over = jnp.where(lane < C, total[...], 0.0) - dot(system[...], adjoint[...], NN, HI)
        adjoint[...] = adjoint[...] + dot(inv[...], left_over, NN, HI)
    start = pl.multiple_of(lax.axis_index("sup") * rows, 8)
    own = pl.ds(start, rows)
    adj = adjoint[...]
    ridge = jnp.sum(jnp.sum(adj * coef_n[...], axis=0, keepdims=True), axis=1, keepdims=True) * (-RIDGE / n_sup)
    row_id = lax.broadcasted_iota(jnp.int32, (rows, n_sup), 0) + start
    col_id = lax.broadcasted_iota(jnp.int32, (rows, n_sup), 1)
    d_kern = jnp.where(row_id == col_id, 2.0 * ridge, 0.0) - dot(adjoint[own, :], coef_t[...], NN, HI)
    d_kern = d_kern - dot(coef_n[own, :], adj, NT, HI)
    weight = d_kern * own_tg[...] * (1.0 / D)
    lane = lax.broadcasted_iota(jnp.int32, (rows, CLS), 1)
    d_norm = jnp.sum(d_kern * own_tr[...], axis=1, keepdims=True)
    d_norm = d_norm + jnp.sum(jnp.where(lane == C + 1, total[own, :], 0.0), axis=1, keepdims=True)
    loss[...] = jnp.sum(jnp.where(lane[0:1] == C, total[0:1, :], 0.0), axis=1, keepdims=True)
    pieces[0:rows] = weight
    pieces[rows:2 * rows] = weight - weight.astype(BF16).astype(F32)
    both = pieces[...].astype(BF16)
    for copy in images_in:
        copy.wait()
    for k in range(D // 512):
        lanes = slice(k * 512, (k + 1) * 512)
        some = dot(both, sup[:, lanes])
        part[:, lanes] = some[:rows] + some[rows:] + (2.0 / D) * d_norm * images[:, lanes].astype(F32)
    receive(third)
    ends[0] = tail[zh] + near_z[0] + (near_z[1] + near_z[2])
    fourth = sender.start(ends.at[0], ends.at[1], beside)
    fourth.wait_recv()
    done[core] = ends[0] + ends[1]
    last = sender.start(done.at[core], done.at[core], partner)
    last.wait_recv()
    for h in range(2):
        lanes = slice(h * half, (h + 1) * half)
        out[:, lanes] = n_sup * (part[:, lanes] + done[h])
    sums.drain()
    sender.drain()


def finish(grad, slab, inv, system, gathered, images, coef_t, coef_n, own_tg, own_tr):
    rows, half, n_sup = images.shape[0], D // 2, inv.shape[0]
    vmem = pl.BlockSpec(memory_space=pltpu.VMEM)
    return pl.pallas_call(
        finish_kernel,
        out_shape=[jax.ShapeDtypeStruct((rows, D), F32), jax.ShapeDtypeStruct((1, 1), F32)],
        in_specs=[vmem] * 4 + [pl.BlockSpec(memory_space=pl.ANY)] + [vmem] * 5,
        out_specs=[vmem] * 2,
        scratch_shapes=[
            pltpu.VMEM((RING, RING, RING, rows, half), BF16),
            pltpu.VMEM((2, 2, RING, rows, half), BF16),
            pltpu.VMEM((2, RING, RING, rows, half), BF16),
            pltpu.VMEM((2, 2, rows, half), BF16),
            pltpu.VMEM((2, RING, rows, half), BF16),
            pltpu.VMEM((RING, rows, half), F32),
            pltpu.VMEM((3, rows, half), F32),
            pltpu.VMEM((2, rows, half), F32),
            pltpu.VMEM((2, rows, half), F32),
            pltpu.VMEM((RING, RING, 2, rows, CLS), F32),
            pltpu.VMEM((3, RING, 2, rows, CLS), F32),
            pltpu.VMEM((3, 2, rows, CLS), F32),
            pltpu.VMEM((8, 2, rows, CLS), F32),
            pltpu.VMEM((2, RING, RING, 2, rows, CLS), F32),
            pltpu.VMEM((n_sup, CLS), F32),
            pltpu.VMEM((n_sup, CLS), F32),
            pltpu.VMEM((n_sup, D), BF16),
            pltpu.VMEM((rows, D), F32),
            pltpu.VMEM((2 * rows, n_sup), F32),
            pltpu.SemaphoreType.DMA((20,)), pltpu.SemaphoreType.DMA((20,)),
            pltpu.SemaphoreType.DMA((24,)), pltpu.SemaphoreType.DMA((24,)),
            pltpu.SemaphoreType.DMA((32,)),
        ],
        compiler_params=pltpu.CompilerParams(
            collective_id=1, has_side_effects=True, vmem_limit_bytes=24 * 2**20),
        name="finish",
    )(
        grad.reshape(2, RING, RING, RING, rows, half), slab.reshape(2, RING, RING, RING, rows, CLS),
        inv, system, gathered, images, coef_t, coef_n, own_tg, own_tr)


def body(support_images, target_images, support_labels, target_labels):
    own_rows = support_images.shape[0]
    lab_s = support_labels.reshape(1, -1)
    lab_t = target_labels.reshape(1, -1)
    gathered, near = gather_images(support_images, target_images)
    gathered = gathered.reshape(2, RING * RING, RING * own_rows, D // 2)
    grad, slab, inv, system, *rest = compute(gathered, near, lab_s, lab_t, own_rows)
    out, loss = finish(grad, slab, inv, system, gathered, support_images, *rest)
    return out, loss[0, 0]


def solution(mesh):
    in_specs = (P("sup", None), P(("tgt", "sup"), None), P(), P(("tgt", "sup")))
    out_specs = (P("sup", None), P())
    return jax.shard_map(body, mesh=mesh, in_specs=in_specs, out_specs=out_specs, check_vma=False)
```

```python
import functools
import math

import jax
import jax.numpy as jnp
from jax import lax
from jax.experimental import pallas as pl
from jax.experimental.pallas import tpu as pltpu
from jax.sharding import PartitionSpec as P

D = 3072
C = 100
LAYERS = 5
CLS = 128
RIDGE = 0.1
TWO_PI = 2.0 / math.pi
NEWTON = 7
NEWTON_TILES = 9
REFINE = 2
HI = lax.Precision.HIGHEST
NN = (((1,), (0,)), ((), ()))
NT = (((1,), (1,)), ((), ()))
F32 = jnp.float32
BF16 = jnp.bfloat16

ASIN = (
    (1.0, 0.1666678637266159, 0.0749453455209732, 0.0455390103161335, 0.02390936389565468, 0.042553599923849106),
    (1.0, 0.1666594296693802, 0.07524710148572922, 0.04152849689126015, 0.04858245328068733, -0.02943584695458412, 0.08121654391288757),
    (1.0, 0.16665531694889069, 0.07537393271923065, 0.04041983559727669, 0.0488600954413414),
    (1.0, 0.16666492819786072, 0.0750882476568222, 0.043096426874399185, 0.04107564687728882),
    (0.9999999403953552, 0.16668136417865753, 0.07438473403453827, 0.052717722952365875),
)


def poly(z, coefs):
    total = coefs[-1] * TWO_PI
    for value in coefs[-2::-1]:
        total = total * z + value * TWO_PI
    return total


def scaled_asin(layer, u, u2):
    if layer > 0:
        return u * poly(u2, ASIN[layer])
    size = jnp.abs(u)
    big = size > 0.5
    z = jnp.where(big, 0.5 - 0.5 * size, u2)
    s = jnp.where(big, z * lax.rsqrt(z), size)
    p = s * poly(z, ASIN[0])
    p = jnp.where(big, 1.0 - 2.0 * p, p)
    return jnp.where(u < 0.0, -p, p)


def norm_layers(p):
    scales, slopes = [], []
    chain = jnp.ones_like(p)
    for layer in range(LAYERS):
        spread = 1.0 + 2.0 * p
        inv = 1.0 / spread
        scales.append(lax.rsqrt(spread))
        slopes.append(chain * inv)
        if layer < LAYERS - 1:
            chain = chain * (2.0 * TWO_PI) * inv * lax.rsqrt(1.0 + 4.0 * p)
            u = 2.0 * p * inv
            p = scaled_asin(layer, u, u * u)
    return scales, slopes


def ntk_value(g, left, right):
    theta = g
    for layer in range(LAYERS):
        c2 = 2.0 * left[layer] * right[layer]
        u = g * c2
        u2 = u * u
        w = lax.rsqrt(1.0 - u2)
        g = scaled_asin(layer, u, u2)
        theta = g + theta * (TWO_PI * c2 * w)
    return theta


def ntk_full(g, left2, right, slope):
    theta = g
    dg = tg = gr = tr = None
    for layer in range(LAYERS):
        last = layer == LAYERS - 1
        c2 = left2[layer] * right[layer]
        u = g * c2
        u2 = u * u
        w = lax.rsqrt(1.0 - u2)
        cw2 = c2 * w
        step = TWO_PI * cw2
        tw = theta * (w * w)
        tb = tw * (u * c2)
        gs = g * slope[layer]
        if layer == 0:
            tg_next = step * (2.0 + tb)
            dg_next = step
            base = -gs
            tr_next = step * (base - tw * slope[layer])
        else:
            tg_next = step * (dg + tg + tb * dg)
            dg_next = step * dg
            base = gr - gs
            tr_next = step * (base + tr + (tb * gr - tw * slope[layer]))
        gr_next = step * base
        g = scaled_asin(layer, u, u2)
        theta = g + step * theta
        tg, dg, gr, tr = tg_next, dg_next, gr_next, tr_next
    return theta, tg, tr


def dot(a, b, dims=NN, precision=None):
    return lax.dot_general(a, b, dims, precision=precision, preferred_element_type=F32)


def split(x):
    high = x.astype(BF16)
    return high, (x - high.astype(F32)).astype(BF16)


def dot3(a, b, dims=NN):
    return dot(a[0], b[0], dims) + (dot(a[0], b[1], dims) + dot(a[1], b[0], dims))


def load_images(gathered, sup, sems):
    half = D // 2
    copies = []
    for y in range(4):
        for x in range(4):
            rows = pl.ds(32 * (y * 4 + x), 32)
            for h, slot in ((0, y * 4 + x), (1, x * 4 + y)):
                dst = sup.at[rows, h * half:(h + 1) * half]
                copies.append(pltpu.make_async_copy(gathered.at[h, slot], dst, sems.at[len(copies)]))
    for copy in copies:
        copy.start()
    return copies


def compute_kernel(
    lab_s, lab_t, gathered, tgt,
    grad, slab, inv, system, coef_t, coef_n, own_tg, own_tr,
    sup, gram, gram_ss, kern, tg_s, tr_s, coef, quant, quant_t, left_s, sq, mid, acc, sems,
):
    for copy in load_images(gathered, sup, sems):
        copy.wait()
    n_sup = sup.shape[0]
    n_tgt = tgt.shape[0]
    total_tgt = n_tgt * lax.axis_size("sup") * lax.axis_size("tgt")
    own_rows = own_tg.shape[0]

    for j in range(n_sup // 256):
        gram_ss[:, j * 256:(j + 1) * 256] = dot(sup[...], sup[j * 256:(j + 1) * 256, :], NT) * (1.0 / D)

    row_id = lax.broadcasted_iota(jnp.int32, (n_sup, n_sup), 0)
    col_id = lax.broadcasted_iota(jnp.int32, (n_sup, n_sup), 1)
    diagonal = row_id == col_id
    norm_s = jnp.sum(jnp.where(diagonal, gram_ss[...], 0.0), axis=0, keepdims=True)
    scales_s, slopes_s = norm_layers(jnp.broadcast_to(norm_s, (8, n_sup)))
    quant[...] = jnp.zeros_like(quant)
    for layer in range(LAYERS):
        quant[layer * 8:layer * 8 + 8, :] = scales_s[layer]
        quant[64 + layer * 8:72 + layer * 8, :] = slopes_s[layer]
    quant_t[...] = quant[...].T

    def ss_tile(i):
        rows = pl.ds(pl.multiple_of(i * 32, 32), 32)
        q = quant_t[rows, :]
        left = [q[:, l * 8:l * 8 + 1] for l in range(LAYERS)]
        right = [quant[l * 8:l * 8 + 1, :] for l in range(LAYERS)]
        system[rows, :] = ntk_value(gram_ss[rows, :], left, right)

    def square_tile(j):
        rows = pl.ds(pl.multiple_of(j * 64, 64), 64)
        total = jnp.zeros((64, 128), F32)
        for k in range(D // 128):
            x = tgt[rows, k * 128:(k + 1) * 128].astype(F32)
            total = total + x * x
        sq[rows, :] = total

    def gram_tile(j, carry):
        rows = pl.ds(pl.multiple_of(j * 256, 256), 256)
        gram[:, rows] = dot(sup[...], tgt[rows, :], NT) * (1.0 / D)
        for i in range(4):
            square_tile(j * 4 + i)
        for i in range(n_sup // 128):
            ss_tile(j * (n_sup // 128) + i)
        return carry

    lax.fori_loop(0, n_tgt // 256, gram_tile, 0)
    norm_t = dot(jnp.full((8, 128), 1.0 / D, F32), sq[...], NT, HI)
    scales_t, unused = norm_layers(norm_t)
    for layer in range(LAYERS):
        left_s[layer] = 2.0 * scales_t[layer]

    def own_tile(i, carry):
        here = pl.ds(pl.multiple_of(i * 8, 8), 8)
        own = pl.ds(pl.multiple_of(lax.axis_index("sup") * own_rows + i * 8, 8), 8)
        q = quant_t[own, :]
        left = [q[:, l * 8:l * 8 + 1] for l in range(LAYERS)]
        slope = [q[:, 64 + l * 8:65 + l * 8] for l in range(LAYERS)]
        right2 = [2.0 * quant[l * 8:l * 8 + 8, :] for l in range(LAYERS)]
        unused, tg, tr = ntk_full(gram_ss[own, :], right2, left, slope)
        own_tg[here, :] = tg
        own_tr[here, :] = tr
        return carry

    lax.fori_loop(0, own_rows // 8, own_tile, 0)

    kern_ss = system[...]
    trace = jnp.sum(jnp.sum(jnp.where(diagonal, kern_ss, 0.0), axis=0, keepdims=True), axis=1, keepdims=True)
    inv_t = n_sup / trace
    system[...] = kern_ss * inv_t + jnp.where(diagonal, RIDGE, 0.0)
    norms = jnp.sum(jnp.abs(system[...]), axis=0, keepdims=True)
    high = jnp.minimum(jnp.max(norms, axis=1, keepdims=True), n_sup + RIDGE)
    alpha = 2.0 / (high + RIDGE)
    rho = (high - RIDGE) / (high + RIDGE)
    gain = 2.0 / (2.0 - rho * rho)
    inv[...] = (gain * alpha) * (jnp.where(diagonal, 2.0, 0.0) - alpha * system[...])
    rho = 0.5 * gain * rho * rho

    half = 512

    def ts_tile(i, j):
        rows = pl.ds(pl.multiple_of(i * 8, 8), 8)
        lanes = pl.ds(j * half, half)
        q = quant_t[rows, :]
        right = [q[:, l * 8:l * 8 + 1] for l in range(LAYERS)]
        slope = [q[:, 64 + l * 8:65 + l * 8] for l in range(LAYERS)]
        left2 = [left_s[l, :, lanes] for l in range(LAYERS)]
        theta, tg, tr = ntk_full(gram[rows, lanes], left2, right, slope)
        kern[rows, lanes] = theta
        tg_s[rows, lanes] = tg
        tr_s[rows, lanes] = tr


    each = NEWTON_TILES

    def newton(k, rho):
        for i in range(each):
            for j in range(n_tgt // half):
                ts_tile(k * each + i, j)
        a = split(system[...])
        x = split(inv[...])
        mid[...] = jnp.where(diagonal, 2.0, 0.0) - dot3(a, x)
        gain = 2.0 / (2.0 - rho * rho)
        inv[...] = gain * dot3(x, split(mid[...]))
        return 0.5 * gain * rho * rho

    lax.fori_loop(0, NEWTON, newton, rho)

    def ts_rest(i, carry):
        for j in range(n_tgt // half):
            ts_tile(i, j)
        return carry

    lax.fori_loop(NEWTON * each, n_sup // 8, ts_rest, 0)
    inv[...] = inv[...] * inv_t
    system[...] = system[...] * (trace * (1.0 / n_sup))

    class_id = lax.broadcasted_iota(jnp.int32, (CLS, n_sup), 0)
    label = jnp.where(class_id == lab_s[...], 1.0, 0.0) - 1.0 / C
    label = jnp.where(class_id < C, label, 0.0)
    coef_t[...] = dot(label, inv[...], NN, HI)
    for k in range(REFINE):
        left_over = label - dot(coef_t[...], system[...], NN, HI)
        coef_t[...] = coef_t[...] + dot(left_over, inv[...], NN, HI)
    coef_n[...] = coef_t[...].T

    class_id = lax.broadcasted_iota(jnp.int32, (CLS, n_tgt), 0)
    label = jnp.where(class_id == lab_t[...], 1.0, 0.0) - 1.0 / C
    label = jnp.where(class_id < C, label, 0.0)
    misfit = dot(coef_t[...], kern[...], NN, HI) - label
    loss = jnp.sum(jnp.sum(misfit * misfit, axis=0, keepdims=True), axis=1, keepdims=True) * (0.5 / total_tgt)
    d_predict = misfit * (1.0 / total_tgt)
    d_coef = dot(kern[...], d_predict, NT, HI)
    gram[...] = dot(coef_n[...], d_predict, NN, HI)

    def pull_tile(i, carry):
        rows = pl.ds(pl.multiple_of(i * 16, 16), 16)
        d_kern = gram[rows, :]
        part = (d_kern * tg_s[rows, :] * (1.0 / D)).astype(BF16)
        coef[0, rows, :] = part
        block = i // 2
        other = (block % 4) * 4 + block // 4
        coef[1, pl.ds(pl.multiple_of(other * 32 + (i % 2) * 16, 16), 16), :] = part
        through = d_kern * tr_s[rows, :]
        total = through[:, :128]
        for k in range(1, n_tgt // 128):
            total = total + through[:, k * 128:(k + 1) * 128]
        acc[rows, :] = total
        return carry

    lax.fori_loop(0, n_sup // 16, pull_tile, 0)
    d_norm = jnp.sum(acc[...], axis=1, keepdims=True)
    lane = lax.broadcasted_iota(jnp.int32, (n_sup, CLS), 1)
    d_coef = jnp.where(lane == C, loss, d_coef)
    acc[...] = jnp.where(lane == C + 1, d_norm, d_coef)
    slab[0] = acc[...]
    for y in range(4):
        for x in range(4):
            slab[1, 32 * (x * 4 + y):32 * (x * 4 + y) + 32, :] = acc[32 * (y * 4 + x):32 * (y * 4 + x) + 32, :]

    for h in range(2):
        def grad_tile(j, carry):
            there = pl.ds(pl.multiple_of(j * 512, 512), 512)
            lanes = pl.ds(pl.multiple_of(j * 512 + h * (D // 2), 512), 512)
            grad[h, :, there] = dot(coef[h], tgt[:, lanes]).astype(grad.dtype)
            return carry

        lax.fori_loop(0, D // 1024, grad_tile, 0)


def compute(gathered, target_images, lab_s, lab_t, own_rows):
    n_sup, n_tgt = gathered.size // D, target_images.shape[0]
    shapes = [
        ((2, n_sup, D // 2), BF16), ((2, n_sup, CLS), F32), ((n_sup, n_sup), F32), ((n_sup, n_sup), F32),
        ((CLS, n_sup), F32), ((n_sup, CLS), F32), ((own_rows, n_sup), F32), ((own_rows, n_sup), F32),
    ]
    vmem = pl.BlockSpec(memory_space=pltpu.VMEM)
    return pl.pallas_call(
        compute_kernel,
        out_shape=[jax.ShapeDtypeStruct(s, t) for s, t in shapes],
        in_specs=[vmem, vmem, pl.BlockSpec(memory_space=pl.ANY), vmem],
        out_specs=[vmem] * len(shapes),
        scratch_shapes=[
            pltpu.VMEM((n_sup, D), BF16),
            pltpu.VMEM((n_sup, n_tgt), F32), pltpu.VMEM((n_sup, n_sup), F32),
            pltpu.VMEM((n_sup, n_tgt), F32), pltpu.VMEM((n_sup, n_tgt), F32), pltpu.VMEM((n_sup, n_tgt), F32),
            pltpu.VMEM((2, n_sup, n_tgt), BF16),
            pltpu.VMEM((128, n_sup), F32), pltpu.VMEM((n_sup, 128), F32),
            pltpu.VMEM((LAYERS, 8, n_tgt), F32), pltpu.VMEM((n_tgt, 128), F32),
            pltpu.VMEM((n_sup, n_sup), F32), pltpu.VMEM((n_sup, 128), F32),
            pltpu.SemaphoreType.DMA((32,)),
        ],
        compiler_params=pltpu.CompilerParams(vmem_limit_bytes=36 * 2**20),
        name="compute",
    )(lab_s, lab_t, gathered, target_images)


MESH = pl.DeviceIdType.MESH
RING = 4


def place():
    tgt, sup = lax.axis_index("tgt"), lax.axis_index("sup")
    core = tgt % 2
    zh = sup % RING
    x = (sup // RING) % RING
    y = sup // (RING * RING)
    a = y + core * (x - y)
    b = x + core * (y - x)
    step_a, step_b = RING - (RING - 1) * core, 1 + (RING - 1) * core

    def device(a_there, b_there, zh_there):
        return (tgt, (a_there * step_a + b_there * step_b) * RING + zh_there)

    partner = (tgt + 1 - 2 * core, sup)
    beside = ((tgt + 2) % 4, sup)
    return core, y, x, a, b, zh, device, partner, beside


def turn(index, by):
    return (index + by) % RING


def greet(devices):
    barrier = pltpu.get_barrier_semaphore()
    for device in devices:
        pl.semaphore_signal(barrier, inc=1, device_id=device, device_id_type=MESH)
    pl.semaphore_wait(barrier, len(devices))


class Sender:
    def __init__(self, send_sems, recv_sems):
        self.send_sems, self.recv_sems, self.made = send_sems, recv_sems, []

    def start(self, src, dst, device):
        k = len(self.made)
        copy = pltpu.make_async_remote_copy(
            src_ref=src, dst_ref=dst, send_sem=self.send_sems.at[k], recv_sem=self.recv_sems.at[k],
            device_id=device, device_id_type=MESH)
        copy.start()
        self.made.append(copy)
        return copy

    def drain(self):
        for copy in self.made:
            copy.wait_send()


def gather_kernel(own, tgt, out, tgt_near, send_sems, recv_sems, local_sem, tgt_sem):
    near = pltpu.make_async_copy(tgt, tgt_near, tgt_sem)
    near.start()
    core, y, x, a, b, zh, device, partner, beside = place()
    greet(
        [device(a, b, turn(zh, k)) for k in (1, 2, 3)]
        + [device(a, turn(b, k), zh) for k in (1, 3)] + [device(turn(a, k), b, zh) for k in (1, 3)] + [partner]
    )
    half = out.shape[-1]
    mine = own.at[:, pl.ds(pl.multiple_of(core * half, 128), half)]
    sender = Sender(send_sems, recv_sems)
    first = [sender.start(mine, out.at[core, a, b, zh], device(a, b, turn(zh, k))) for k in (1, 3, 2)]
    local = pltpu.make_async_copy(mine, out.at[core, a, b, zh], local_sem)
    local.start()
    local.wait()
    for copy in first:
        copy.wait_recv()
    low, high = pl.ds(0, 2), pl.ds(2, 2)
    left_a, right_a = device(turn(a, 3), b, zh), device(turn(a, 1), b, zh)
    left_b, right_b = device(a, turn(b, 3), zh), device(a, turn(b, 1), zh)
    across = []

    def share(ref):
        across.append(sender.start(ref, ref, partner))

    def block(k, m):
        return out.at[core, turn(a, k), turn(b, m)]

    def send(ref, there):
        return sender.start(ref, ref, there)

    along_a = {}

    def launch(m):
        along_a[m] = (send(block(0, m), right_a), send(block(0, m), left_a))

    b_right, b_left = send(block(0, 0), right_b), send(block(0, 0), left_b)
    launch(0)
    share(block(0, 0))
    b_right.wait_recv()
    far_right = send(block(0, 3).at[low], right_b)
    launch(3)
    share(block(0, 3))
    b_left.wait_recv()
    far_left = send(block(0, 1).at[high], left_b)
    launch(1)
    share(block(0, 1))
    far_right.wait_recv()
    far_left.wait_recv()
    launch(2)
    share(block(0, 2))
    last = {}
    for m in (0, 3, 1, 2):
        to_right, to_left = along_a[m]
        to_right.wait_recv()
        first_half = send(block(3, m).at[low], right_a)
        share(block(3, m))
        to_left.wait_recv()
        last[m] = (first_half, send(block(1, m).at[high], left_a))
        share(block(1, m))
    for m in (0, 3, 1, 2):
        for copy in last[m]:
            copy.wait_recv()
        share(block(2, m))
    for copy in across:
        copy.wait_recv()
    sender.drain()
    near.wait()


def gather_images(support_images, target_images):
    rows = support_images.shape[0]
    return pl.pallas_call(
        gather_kernel,
        out_shape=[
            jax.ShapeDtypeStruct((2, RING, RING, RING, rows, D // 2), BF16),
            jax.ShapeDtypeStruct(target_images.shape, BF16),
        ],
        in_specs=[pl.BlockSpec(memory_space=pl.ANY)] * 2,
        out_specs=[pl.BlockSpec(memory_space=pl.ANY)] * 2,
        scratch_shapes=[pltpu.SemaphoreType.DMA((40,)), pltpu.SemaphoreType.DMA((40,)), pltpu.SemaphoreType.DMA,
            pltpu.SemaphoreType.DMA],
        compiler_params=pltpu.CompilerParams(
            collective_id=0, has_side_effects=True, vmem_limit_bytes=41 * 2**20),
        cost_estimate=pl.CostEstimate(flops=0, bytes_accessed=80 * 2**20, transcendentals=0),
        name="gather",
    )(support_images, target_images)


def add_blocks(dst, parts, lead):
    count = math.prod(lead)

    def one(t, carry):
        index = []
        for length in reversed(lead):
            index.append(t % length)
            t = t // length
        index = tuple(reversed(index))
        if len(parts) == 1:
            dst[index] = dst[index] + parts[0][index]
            return carry
        total = dst[index].astype(F32)
        for part in parts:
            total = total + part[index].astype(F32)
        dst[index] = total.astype(dst.dtype)
        return carry

    lax.fori_loop(0, count, one, 0)


def ring_scatter_start(sender, near, block, me, left, right):
    far = block(turn(me, 2))
    to_right = sender.start(far.at[pl.ds(0, 2)], near.at[0], right)
    to_left = sender.start(far.at[pl.ds(2, 2)], near.at[1], left)
    return to_right, to_left


def ring_scatter_early(sender, landing, block, me, left, right):
    after, before = block(turn(me, 1)), block(turn(me, 3))
    low, high = pl.ds(0, 2), pl.ds(2, 2)
    return [
        sender.start(after.at[high], landing.at[0, high], right),
        sender.start(before.at[low], landing.at[1, low], left),
    ]


def ring_scatter_middle(sender, near, landing, block, me, left, right, copies, lead):
    to_right, to_left = copies
    low, high = pl.ds(0, 2), pl.ds(2, 2)
    after, before = block(turn(me, 1)), block(turn(me, 3))
    to_right.wait_recv()
    add_blocks(after.at[pl.ds(0, 2)], [near.at[0]], lead)
    second_right = sender.start(after.at[low], landing.at[0, low], right)
    to_left.wait_recv()
    add_blocks(before.at[pl.ds(2, 2)], [near.at[1]], lead)
    second_left = sender.start(before.at[high], landing.at[1, high], left)
    return second_right, second_left


def receive(copies):
    for copy in copies:
        copy.wait_recv()


def finish_kernel(
    grad, slab, inv, system, gathered, images, coef_t, coef_n, own_tg, own_tr,
    out, loss,
    work, near_a, far_a, near_b, far_b, tail, near_z, ends, done,
    sum_work, sum_a, sum_b, sum_z, sum_all, total, adjoint,
    sup, part, pieces,
    send_sems, recv_sems, sum_send, sum_recv, sup_sems,
):
    core, y, x, a, b, zh, device, partner, beside = place()
    tgt_id = lax.axis_index("tgt")
    place_z = zh * 2 + tgt_id // 2

    def along_z(k):
        there = (place_z + k) % 8
        return ((there % 2) * 2 + core, (y * RING + x) * RING + there // 2)

    rows = images.shape[0]
    n_sup = inv.shape[0]
    half = D // 2
    images_in = load_images(gathered, sup, sup_sems)
    greet(
        [device(turn(a, k), b, zh) for k in (1, 2, 3)] + [device(a, turn(b, k), zh) for k in (1, 2, 3)]
        + [along_z(k) for k in range(1, 8)] + [partner]
    )
    sums = Sender(sum_send, sum_recv)
    sender = Sender(send_sems, recv_sems)
    left_a, right_a = device(turn(a, 3), b, zh), device(turn(a, 1), b, zh)
    left_b, right_b = device(a, turn(b, 3), zh), device(a, turn(b, 1), zh)

    pair_sum = sums.start(slab.at[1 - core, :, :, pl.ds(2 - 2 * core, 2)], sum_work, partner)
    pair = {}
    for k in (2, 1, 3, 0):
        there = turn(b, k)
        pair[k] = sender.start(grad.at[1 - core, there], work.at[there], partner)

    def add_pair(k):
        pair[k].wait_recv()
        here = turn(a, k)
        add_blocks(work.at[here], [grad.at[core, here]], (RING,))

    def at_a(i):
        return work.at[i]

    def at_b(i):
        return work.at[a, i]

    pair_sum.wait_recv()
    sum_work[...] = sum_work[...] + slab[core, :, :, pl.ds(2 * core, 2)]
    hop = [sums.start(sum_work.at[turn(a, k)], sum_a.at[k - 1], device(turn(a, k), b, zh)) for k in (2, 1, 3)]
    add_pair(2)
    first = ring_scatter_start(sender, near_a, at_a, a, left_a, right_a)
    receive(hop)
    sum_work[a] = sum_work[a] + sum_a[0] + sum_a[1] + sum_a[2]
    hop = [sums.start(sum_work.at[a, turn(b, k)], sum_b.at[k - 1], device(a, turn(b, k), zh)) for k in (2, 1, 3)]
    add_pair(1)
    add_pair(3)
    early = ring_scatter_early(sender, far_a, at_a, a, left_a, right_a)
    receive(hop)
    sum_z[place_z] = sum_work[a, b] + sum_b[0] + sum_b[1] + sum_b[2]
    hop = [sums.start(sum_z.at[place_z], sum_z.at[place_z], along_z(k)) for k in range(1, 8)]
    second = ring_scatter_middle(sender, near_a, far_a, at_a, a, left_a, right_a, first, (2,))
    receive(hop)
    whole = sum_z[0]
    for k in range(1, 8):
        whole = whole + sum_z[k]
    sum_all[core, a, b] = whole
    spot = sum_all.at[core, a, b]
    hop = [sums.start(spot, spot, device(a, turn(b, k), zh)) for k in (2, 1, 3)]
    add_pair(0)
    receive(hop)
    spot = sum_all.at[core, a]
    hop = [sums.start(spot, spot, device(turn(a, k), b, zh)) for k in (2, 1, 3)]
    receive(hop)
    spot = sum_all.at[core]
    pair_sum = sums.start(spot, spot, partner)
    receive(early)
    receive(second)

    def add_a(k):
        here = turn(b, k)
        add_blocks(work.at[a, here], [far_a.at[0, here], far_a.at[1, here]], (RING,))

    add_a(2)
    first = ring_scatter_start(sender, near_b, at_b, b, left_b, right_b)
    add_a(1)
    add_a(3)
    early = ring_scatter_early(sender, far_b, at_b, b, left_b, right_b)
    add_a(0)
    pair_sum.wait_recv()

    for i in range(RING):
        for j in range(RING):
            base = 4 * rows * (i * RING + j)
            total[base:base + 2 * rows, :] = sum_all[0, i, j].reshape(2 * rows, CLS)
            total[base + 2 * rows:base + 4 * rows, :] = sum_all[1, j, i].reshape(2 * rows, CLS)
    lane = lax.broadcasted_iota(jnp.int32, (n_sup, CLS), 1)
    adjoint[...] = dot(inv[...], jnp.where(lane < C, total[...], 0.0), NN, HI)
    second = ring_scatter_middle(sender, near_b, far_b, at_b, b, left_b, right_b, first, ())
    left_over = jnp.where(lane < C, total[...], 0.0) - dot(system[...], adjoint[...], NN, HI)
    adjoint[...] = adjoint[...] + dot(inv[...], left_over, NN, HI)
    receive(early)
    receive(second)
    for i in range(RING):
        tail[i] = work[a, b, i].astype(F32) + far_b[0, i].astype(F32) + far_b[1, i].astype(F32)
    third = [sender.start(tail.at[turn(zh, k)], near_z.at[k - 1], device(a, b, turn(zh, k))) for k in (2, 1, 3)]
    for k in range(REFINE - 1):
        left_over = jnp.where(lane < C, total[...], 0.0) - dot(system[...], adjoint[...], NN, HI)
        adjoint[...] = adjoint[...] + dot(inv[...], left_over, NN, HI)
    start = pl.multiple_of(lax.axis_index("sup") * rows, 8)
    own = pl.ds(start, rows)
    adj = adjoint[...]
    ridge = jnp.sum(jnp.sum(adj * coef_n[...], axis=0, keepdims=True), axis=1, keepdims=True) * (-RIDGE / n_sup)
    row_id = lax.broadcasted_iota(jnp.int32, (rows, n_sup), 0) + start
    col_id = lax.broadcasted_iota(jnp.int32, (rows, n_sup), 1)
    d_kern = jnp.where(row_id == col_id, 2.0 * ridge, 0.0) - dot(adjoint[own, :], coef_t[...], NN, HI)
    d_kern = d_kern - dot(coef_n[own, :], adj, NT, HI)
    weight = d_kern * own_tg[...] * (1.0 / D)
    lane = lax.broadcasted_iota(jnp.int32, (rows, CLS), 1)
    d_norm = jnp.sum(d_kern * own_tr[...], axis=1, keepdims=True)
    d_norm = d_norm + jnp.sum(jnp.where(lane == C + 1, total[own, :], 0.0), axis=1, keepdims=True)
    loss[...] = jnp.sum(jnp.where(lane[0:1] == C, total[0:1, :], 0.0), axis=1, keepdims=True)
    pieces[0:rows] = weight
    pieces[rows:2 * rows] = weight - weight.astype(BF16).astype(F32)
    both = pieces[...].astype(BF16)
    for copy in images_in:
        copy.wait()
    for k in range(D // 512):
        lanes = slice(k * 512, (k + 1) * 512)
        some = dot(both, sup[:, lanes])
        part[:, lanes] = some[:rows] + some[rows:] + (2.0 / D) * d_norm * images[:, lanes].astype(F32)
    receive(third)
    ends[0] = tail[zh] + near_z[0] + (near_z[1] + near_z[2])
    fourth = sender.start(ends.at[0], ends.at[1], beside)
    fourth.wait_recv()
    done[core] = ends[0] + ends[1]
    last = sender.start(done.at[core], done.at[core], partner)
    last.wait_recv()
    for h in range(2):
        lanes = slice(h * half, (h + 1) * half)
        out[:, lanes] = n_sup * (part[:, lanes] + done[h])
    sums.drain()
    sender.drain()


def finish(grad, slab, inv, system, gathered, images, coef_t, coef_n, own_tg, own_tr):
    rows, half, n_sup = images.shape[0], D // 2, inv.shape[0]
    vmem = pl.BlockSpec(memory_space=pltpu.VMEM)
    return pl.pallas_call(
        finish_kernel,
        out_shape=[jax.ShapeDtypeStruct((rows, D), F32), jax.ShapeDtypeStruct((1, 1), F32)],
        in_specs=[vmem] * 4 + [pl.BlockSpec(memory_space=pl.ANY)] + [vmem] * 5,
        out_specs=[vmem] * 2,
        scratch_shapes=[
            pltpu.VMEM((RING, RING, RING, rows, half), BF16),
            pltpu.VMEM((2, 2, RING, rows, half), BF16),
            pltpu.VMEM((2, RING, RING, rows, half), BF16),
            pltpu.VMEM((2, 2, rows, half), BF16),
            pltpu.VMEM((2, RING, rows, half), BF16),
            pltpu.VMEM((RING, rows, half), F32),
            pltpu.VMEM((3, rows, half), F32),
            pltpu.VMEM((2, rows, half), F32),
            pltpu.VMEM((2, rows, half), F32),
            pltpu.VMEM((RING, RING, 2, rows, CLS), F32),
            pltpu.VMEM((3, RING, 2, rows, CLS), F32),
            pltpu.VMEM((3, 2, rows, CLS), F32),
            pltpu.VMEM((8, 2, rows, CLS), F32),
            pltpu.VMEM((2, RING, RING, 2, rows, CLS), F32),
            pltpu.VMEM((n_sup, CLS), F32),
            pltpu.VMEM((n_sup, CLS), F32),
            pltpu.VMEM((n_sup, D), BF16),
            pltpu.VMEM((rows, D), F32),
            pltpu.VMEM((2 * rows, n_sup), F32),
            pltpu.SemaphoreType.DMA((24,)), pltpu.SemaphoreType.DMA((24,)),
            pltpu.SemaphoreType.DMA((24,)), pltpu.SemaphoreType.DMA((24,)),
            pltpu.SemaphoreType.DMA((32,)),
        ],
        compiler_params=pltpu.CompilerParams(
            collective_id=1, has_side_effects=True, vmem_limit_bytes=24 * 2**20),
        name="finish",
    )(
        grad.reshape(2, RING, RING, RING, rows, half), slab.reshape(2, RING, RING, RING, rows, CLS),
        inv, system, gathered, images, coef_t, coef_n, own_tg, own_tr)


def body(support_images, target_images, support_labels, target_labels):
    own_rows = support_images.shape[0]
    lab_s = support_labels.reshape(1, -1)
    lab_t = target_labels.reshape(1, -1)
    gathered, near = gather_images(support_images, target_images)
    gathered = gathered.reshape(2, RING * RING, RING * own_rows, D // 2)
    grad, slab, inv, system, *rest = compute(gathered, near, lab_s, lab_t, own_rows)
    out, loss = finish(grad, slab, inv, system, gathered, support_images, *rest)
    return out, loss[0, 0]


def solution(mesh):
    in_specs = (P("sup", None), P(("tgt", "sup"), None), P(), P(("tgt", "sup")))
    out_specs = (P("sup", None), P())
    return jax.shard_map(body, mesh=mesh, in_specs=in_specs, out_specs=out_specs, check_vma=False)
```
